128 devices in a mesh: segment: 4 (over x), dp: 32 (over y, z, core).
Axes of the slice: x: 4, y: 4, z: 4, core: 2. Of those that a mesh axis runs over, the one named last changes fastest.
Arguments:
- images: bfloat16 [128, 16, 16, 512], P('dp'), may hold values from -6 to 6
- labels: int32 [128], P('dp'), may hold values from 0 to 999
- counts: int32 [4], replicated, may hold values from 1 to 4, as said below
- depthwise: bfloat16 [16, 9, 512], P('segment'), may hold values from -2 to 2
- pointwise: bfloat16 [16, 512, 512], P('segment'), may hold values from -0.09375 to 0.09375
- head_weight: float32 [512, 1000], replicated, may hold values from -0.25 to 0.25
Outputs:
- grad_pointwise: float32 [16, 512, 512], P('segment', 'dp')
- grad_depthwise: float32 [16, 9, 512], P('segment', None, 'dp')
The draws below stay inside these ranges and needn't reach their ends.
Inputs may be any that keep to these rules, and one draw needn't show every extreme that they name: Section s runs its first counts[s] cell slots; some section runs all 4 and another a single cell.
All inputs are finite; a program needn't handle non-finite values.
Results may differ from the reference program's by a relative error of at most 0.00085.
Values may be sent and summed in bfloat16 or wider, within the bound.
No kernel may reach another device: no remote copies, remote signals or barrier semaphores. Data moves between devices by JAX's collectives and lax.ppermute only.
A program may use at most 128 MiB of HBM per device.

```python
import jax
import jax.numpy as jnp
from jax import lax

CHAN = 512
CLASSES = 1000
SIDE = 16
CELLS = 4
MICRO = 4
BATCH_MB = 1
IMAGES = 128
SLOTS = 16
N_SEGMENT = 4
N_DP = 32


def draw_counts(key, part):
    first_key = jax.random.fold_in(key, 11)
    second_key = jax.random.fold_in(key, 23)
    values = jax.random.randint(first_key, (N_SEGMENT,), 1, CELLS + 1)
    fullest = jax.random.randint(second_key, (), 0, N_SEGMENT)
    segments = jnp.arange(N_SEGMENT, dtype=jnp.int32)
    values = jnp.where(segments == fullest, CELLS, values)
    values = jnp.where(segments == (fullest + 1) % N_SEGMENT, 1, values)
    return values.astype(jnp.int32)


def touch_ends(values, rng, smallest, largest):
    index_at = [jax.random.randint(jax.random.fold_in(rng, axis), (), 0, length) for axis, length in enumerate(values.shape)]
    widest = values.shape.index(max(values.shape))
    neighbour = index_at[:widest] + [(index_at[widest] + 1) % values.shape[widest]] + index_at[widest + 1:]
    return values.at[tuple(index_at)].set(smallest).at[tuple(neighbour)].set(largest)


def level_of(own_key, dims, shards, least, top_value):
    gain = 1.0
    for position, parts in shards:
        heights = jax.random.uniform(jax.random.fold_in(jax.random.fold_in(own_key, 6), position), (parts,), jnp.float32, least / len(shards), top_value / len(shards))
        gain = gain * jnp.repeat(jnp.exp(heights), dims[position] // parts).reshape((-1,) + (1,) * (len(dims) - 1 - position))
    return gain


def noise(own_key, shape, deviation, reach, pieces=(), kind=jnp.bfloat16):
    factor_of = level_of(own_key, shape, pieces, -0.22, 0.18) if pieces else 1.0
    entries = jax.random.normal(own_key, shape, jnp.float32) * deviation * factor_of
    return jnp.minimum(jnp.maximum(entries, -reach), reach).astype(kind)


def setup_inputs(seed: int = 0) -> dict:
    arg_keys = jax.random.split(jax.random.key(seed), 7)
    return {
        "images": noise(arg_keys[0], (IMAGES, SIDE, SIDE, CHAN), 1.0, 6.0, ((0, 32),)),
        "labels": touch_ends(jax.random.randint(arg_keys[1], (IMAGES,), 0, CLASSES), jax.random.fold_in(arg_keys[1], 1), 0, CLASSES - 1).astype(jnp.int32),
        "counts": draw_counts(jax.random.fold_in(arg_keys[6], 71), 0),
        "depthwise": noise(arg_keys[3], (SLOTS, 9, CHAN), 9 ** -0.5, 2.0, ((0, 4),)),
        "pointwise": noise(arg_keys[4], (SLOTS, CHAN, CHAN), (8 * CHAN) ** -0.5, 0.09375, ((0, 4),)),
        "head_weight": noise(arg_keys[5], (CHAN, CLASSES), CHAN ** -0.5, 0.25, (), jnp.float32),
    }


def offsets(dilation):
    return [(row * dilation, col * dilation) for row in (-1, 0, 1) for col in (-1, 0, 1)]

def shifted_view(field, shift_row, shift_col):
    side = field.shape[1]
    padded = jnp.pad(field, ((0, 0), (2, 2), (2, 2), (0, 0)))
    return padded[:, 2 + shift_row:2 + shift_row + side, 2 + shift_col:2 + shift_col + side, :]

def depth_mix(relu_field, kernel, dilation):
    kernel_wide = kernel.astype(jnp.float32)
    mixed = jnp.zeros(relu_field.shape, jnp.float32)
    for tap_index, (shift_row, shift_col) in enumerate(offsets(dilation)):
        mixed = mixed + shifted_view(relu_field, shift_row, shift_col).astype(jnp.float32) * kernel_wide[tap_index]
    return mixed.astype(jnp.bfloat16)

def cell_forward(field, kernel, weight, dilation):
    relu_field = jnp.maximum(field, jnp.zeros((), field.dtype))
    spread = depth_mix(relu_field, kernel, dilation)
    width = field.shape[3]
    projected = jnp.dot(spread.reshape(-1, width), weight, preferred_element_type=jnp.float32).reshape(field.shape)
    return (field.astype(jnp.float32) + projected).astype(jnp.bfloat16)

def cell_backward(field, cotangent, kernel, weight, dilation):
    width = field.shape[3]
    relu_field = jnp.maximum(field, jnp.zeros((), field.dtype))
    spread = depth_mix(relu_field, kernel, dilation)
    flat_grad = cotangent.reshape(-1, width)
    grad_weight = lax.dot_general(spread.reshape(-1, width), flat_grad, (((0,), (0,)), ((), ())), preferred_element_type=jnp.float32)
    grad_spread = lax.dot_general(flat_grad, weight, (((1,), (1,)), ((), ())), preferred_element_type=jnp.float32)
    spread_wide = grad_spread.astype(jnp.bfloat16).reshape(field.shape).astype(jnp.float32)
    kernel_wide = kernel.astype(jnp.float32)
    kernel_rows = []
    back_sum = jnp.zeros(field.shape, jnp.float32)
    for tap_index, (shift_row, shift_col) in enumerate(offsets(dilation)):
        kernel_rows.append(lax.optimization_barrier(jnp.sum(spread_wide * shifted_view(relu_field, shift_row, shift_col).astype(jnp.float32), axis=(0, 1, 2))))
        back_sum = back_sum + shifted_view(spread_wide, -shift_row, -shift_col) * kernel_wide[tap_index]
    grad_kernel = jnp.stack(kernel_rows)
    grad_in = (cotangent.astype(jnp.float32) + jnp.where(field > 0, back_sum, jnp.zeros((), jnp.float32))).astype(jnp.bfloat16)
    return (grad_in, grad_weight, grad_kernel)

def head_grad(final, head_weight, label_row, image_total):
    pooled = lax.optimization_barrier(jnp.mean(final.astype(jnp.float32), axis=(1, 2)))
    logits = jnp.dot(pooled, head_weight, precision=lax.Precision.HIGHEST, preferred_element_type=jnp.float32)
    classes = jnp.arange(head_weight.shape[1], dtype=jnp.int32)
    target = (label_row[:, None] == classes[None, :]).astype(jnp.float32)
    error_term = (jax.nn.sigmoid(logits) - target) / image_total
    back_pool = jnp.dot(error_term, head_weight.T, precision=lax.Precision.HIGHEST, preferred_element_type=jnp.float32)
    back_pool = back_pool / (final.shape[1] * final.shape[2])
    return jnp.broadcast_to(back_pool[:, None, None, :], final.shape).astype(jnp.bfloat16)

def reference(images, labels, counts, depthwise, pointwise, head_weight):
    slot_total = depthwise.shape[0]
    per_segment = slot_total // N_SEGMENT
    image_total = N_DP * MICRO * BATCH_MB
    batches = images.reshape(N_DP * MICRO, BATCH_MB, SIDE, SIDE, CHAN)
    label_rows = labels.reshape(N_DP * MICRO, BATCH_MB)
    live_slots = [counts[slot // per_segment] > slot % per_segment for slot in range(slot_total)]

    def one_micro(running, micro_item):
        weight_sums, kernel_sums = running
        field, label_row = micro_item
        inputs = []
        for slot in range(slot_total):
            inputs.append(field)
            result = cell_forward(field, depthwise[slot], pointwise[slot], 1 + slot % per_segment % 2)
            field = jnp.where(live_slots[slot], result, field)
        cotangent = head_grad(field, head_weight, label_row, image_total)
        weight_list = [None] * slot_total
        kernel_list = [None] * slot_total
        for slot in reversed(range(slot_total)):
            grad_in, grad_weight, grad_kernel = cell_backward(inputs[slot], cotangent, depthwise[slot], pointwise[slot], 1 + slot % per_segment % 2)
            weight_list[slot] = jnp.where(live_slots[slot], grad_weight, jnp.zeros((), jnp.float32))
            kernel_list[slot] = jnp.where(live_slots[slot], grad_kernel, jnp.zeros((), jnp.float32))
            cotangent = jnp.where(live_slots[slot], grad_in, cotangent)
        return ((weight_sums + jnp.stack(weight_list), kernel_sums + jnp.stack(kernel_list)), None)
    zeros_init = (jnp.zeros(pointwise.shape, jnp.float32), jnp.zeros(depthwise.shape, jnp.float32))
    (weight_sums, kernel_sums), unused = lax.scan(one_micro, zeros_init, (batches, label_rows))
    return (weight_sums, kernel_sums)
```

```python
import functools

import jax
import jax.numpy as jnp
from jax import lax
from jax.experimental import pallas as pl
from jax.experimental.pallas import tpu as pltpu
from jax.sharding import PartitionSpec as P

F32 = jnp.float32
BF16 = jnp.bfloat16
SIDE, POS, CHAN, LANE, CLASSES = 16, 256, 512, 128, 1000
TAPS = [(a, b) for a in (-1, 0, 1) for b in (-1, 0, 1)]
WROWS = CHAN + 16
ROWS = 128
GD_ROWS = 16


def step_kernel(info, images, own, r1, r2, r3, e1, e2, e3, head, out0, out1,
                wv, xs, us, pad, dyb, gw, gdb, gdt, hv, wsem, isem, hsem, gsem, tsem):
    seg, core, my_y, my_z, label = (info[4], info[5], info[6], info[7], info[8])
    copies = [pltpu.make_async_copy(own, wv.at[seg], wsem.at[seg, 0])]
    for k, (near, far) in enumerate(((r1, e1), (r2, e2), (r3, e3)), 1):
        section = lax.rem(seg + 4 - k, 4)
        copies.append(pltpu.make_async_copy(near, wv.at[section, pl.ds(2 * core, 2)], wsem.at[section, 0]))
        copies.append(pltpu.make_async_copy(far, wv.at[section, pl.ds(2 - 2 * core, 2)], wsem.at[section, 1]))
    image_copy = pltpu.make_async_copy(images.at[seg], xs.at[0], isem)
    head_copy = pltpu.make_async_copy(head, hv, hsem)
    image_copy.start()
    for copy in copies:
        copy.start()
    head_copy.start()
    pad[...] = jnp.zeros(pad.shape, F32)
    gdb[...] = jnp.zeros(gdb.shape, F32)
    for copy in copies:
        copy.wait()
    image_copy.wait()

    def live_base(section):
        base = jnp.int32(0)
        for s in range(3):
            base = base + jnp.where(s < section, info[s], 0)
        return base

    def lanes(cb):
        return pl.ds(pl.multiple_of(cb * LANE, LANE), LANE)

    def forward_cell(section, slot, n, dil):
        def block(cb, carry):
            field = xs[n, :, lanes(cb)].astype(F32)
            pad[cb, 2:18, 8:24, :] = jnp.maximum(field, 0.0).reshape(SIDE, SIDE, LANE)
            taps = wv[section, slot, CHAN:WROWS, lanes(cb)].astype(F32)
            for rb in range(4):
                mixed = jnp.zeros((4, SIDE, LANE), F32)
                for t, (a, b) in enumerate(TAPS):
                    view = pad[cb, 2 + 4 * rb + a * dil:6 + 4 * rb + a * dil, 8 + b * dil:24 + b * dil, :]
                    mixed = mixed + view * taps[t]
                us[n, 64 * rb:64 * rb + 64, lanes(cb)] = mixed.reshape(64, LANE).astype(BF16)
            return carry
        lax.fori_loop(0, 4, block, 0)
        y = jnp.dot(us[n], wv[section, slot, 0:CHAN, :], preferred_element_type=F32)
        xs[n + 1] = (xs[n].astype(F32) + y).astype(BF16)

    def forward_pair(p, carry):
        section = p // 2
        base = live_base(section)
        for par in range(2):
            slot = 2 * lax.rem(p, 2) + par

            @pl.when(slot < info[section])
            def _():
                forward_cell(section, slot, base + slot, 1 + par)
        return carry

    lax.fori_loop(0, 8, forward_pair, 0)

    total = info[0] + info[1] + info[2] + info[3]
    head_copy.wait()
    final = xs[total].astype(F32)
    pooled = jnp.broadcast_to(jnp.sum(final, axis=0, keepdims=True) / POS, (8, CHAN))
    logits = jnp.dot(pooled, hv[...], precision=lax.Precision.HIGHEST, preferred_element_type=F32)
    classes = lax.broadcasted_iota(jnp.int32, (8, CLASSES), 1)
    target = jnp.where(classes == label, 1.0, 0.0)
    err = (jax.nn.sigmoid(logits) - target) / 128
    back = lax.dot_general(err, hv[...], (((1,), (1,)), ((), ())), precision=lax.Precision.HIGHEST,
                           preferred_element_type=F32) / POS
    dyb[...] = jnp.broadcast_to(back[0:1], (POS, CHAN)).astype(BF16)

    def backward_cell(section, slot, n, dil, par):
        dy = dyb[...]
        gw[par] = lax.dot_general(us[n], dy, (((0,), (0,)), ((), ())), preferred_element_type=F32)
        du = lax.dot_general(dy, wv[section, slot, 0:CHAN, :], (((1,), (1,)), ((), ())), preferred_element_type=F32)
        du = du.astype(BF16).astype(F32)
        for cb in range(4):
            pad[cb, 2:18, 8:24, :] = du[:, cb * LANE:cb * LANE + LANE].reshape(SIDE, SIDE, LANE)

        def block(cb, carry):
            taps = wv[section, slot, CHAN:WROWS, lanes(cb)].astype(F32)
            sums = [jnp.zeros((SIDE, LANE), F32) for _ in TAPS]
            for rb in range(4):
                x = xs[n, 64 * rb:64 * rb + 64, lanes(cb)].astype(F32)
                r = jnp.maximum(x, 0.0).reshape(4, SIDE, LANE)
                acc = jnp.zeros((4, SIDE, LANE), F32)
                for t, (a, b) in enumerate(TAPS):
                    view = pad[cb, 2 + 4 * rb - a * dil:6 + 4 * rb - a * dil, 8 - b * dil:24 - b * dil, :]
                    acc = acc + view * taps[t]
                    sums[t] = sums[t] + jnp.sum(view * r, axis=0)
                old = dyb[64 * rb:64 * rb + 64, lanes(cb)].astype(F32)
                dyb[64 * rb:64 * rb + 64, lanes(cb)] = (
                    old + jnp.where(x > 0, acc.reshape(64, LANE), 0.0)).astype(BF16)
            rows = [jnp.sum(v, axis=0, keepdims=True) for v in sums]
            rows.append(jnp.zeros((7, LANE), F32))
            gdb[pl.ds(pl.multiple_of(slot * 16, 16), 16), lanes(cb)] = jnp.concatenate(rows, axis=0)
            return carry
        lax.fori_loop(0, 4, block, 0)

    outs = (out0, out1)

    def target_of(par, d):
        y, z, c = d // 8, lax.rem(d // 2, 4), lax.rem(d, 2)
        ry, rz, rc = lax.rem(y + 4 - my_y, 4), lax.rem(z + 4 - my_z, 4), jnp.bitwise_xor(c, core)
        return (rc, ry, rz) if par == 0 else (rc, rz, ry)

    def send_slot(par, section, slot):
        def one(d, carry):
            row = pl.multiple_of((section * 2 + slot // 2) * 16, 16)
            i, j, k = target_of(par, d)
            pltpu.make_async_copy(gw.at[par, pl.ds(pl.multiple_of(d * 16, 16), 16)],
                                  outs[par].at[i, j, k, pl.ds(row, 16)], gsem.at[par]).start()
            return carry
        lax.fori_loop(0, 32, one, 0)

    def send_taps(section):
        def one(d, carry):
            i, j, k = target_of(0, d)
            pltpu.make_async_copy(gdt.at[section, pl.ds(pl.multiple_of(d * 16, 16), 16)],
                                  out0.at[i, j, k, pl.ds(ROWS, GD_ROWS), lanes(section)], tsem).start()
            return carry
        lax.fori_loop(0, 32, one, 0)

    def drain(par):
        pltpu.make_async_copy(gw.at[par], gw.at[par], gsem.at[par]).wait()

    def backward_pair(q, carry):
        p = 7 - q
        section = p // 2
        base = live_base(section)
        for par in (1, 0):
            slot = 2 * lax.rem(p, 2) + par
            live = slot < info[section]

            @pl.when(q > 0)
            def _():
                drain(par)

            @pl.when(live)
            def _():
                backward_cell(section, slot, base + slot, 1 + par, par)

            @pl.when(jnp.logical_not(live))
            def _():
                gw[par] = jnp.zeros((CHAN, CHAN), F32)
                gdb[pl.ds(pl.multiple_of(slot * 16, 16), 16), :] = jnp.zeros((16, CHAN), F32)
            send_slot(par, section, slot)

        @pl.when(lax.rem(p, 2) == 0)
        def _():
            gdt[section] = jnp.transpose(gdb[...])
            send_taps(section)
        return carry

    lax.fori_loop(0, 8, backward_pair, 0)
    drain(1)
    drain(0)
    pltpu.make_async_copy(gdt, gdt, tsem).wait()


def run_step(info, images, parts, head):
    hbm = pl.BlockSpec(memory_space=pl.ANY)
    return pl.pallas_call(
        step_kernel,
        in_specs=[pl.BlockSpec(memory_space=pltpu.SMEM)] + [hbm] * 9,
        out_specs=[hbm, hbm],
        out_shape=[jax.ShapeDtypeStruct((2, 4, 4, ROWS + GD_ROWS, CHAN), F32),
                   jax.ShapeDtypeStruct((2, 4, 4, ROWS, CHAN), F32)],
        scratch_shapes=[
            pltpu.VMEM((4, 4, WROWS, CHAN), BF16),
            pltpu.VMEM((17, POS, CHAN), BF16),
            pltpu.VMEM((16, POS, CHAN), BF16),
            pltpu.VMEM((4, 20, 32, LANE), F32),
            pltpu.VMEM((POS, CHAN), BF16),
            pltpu.VMEM((2, CHAN, CHAN), F32),
            pltpu.VMEM((LANE, CHAN), F32),
            pltpu.VMEM((4, CHAN, LANE), F32),
            pltpu.VMEM((CHAN, CLASSES), F32),
            pltpu.SemaphoreType.DMA((4, 2)),
            pltpu.SemaphoreType.DMA,
            pltpu.SemaphoreType.DMA,
            pltpu.SemaphoreType.DMA((2,)),
            pltpu.SemaphoreType.DMA,
        ],
        compiler_params=pltpu.CompilerParams(vmem_limit_bytes=56 * 1024 * 1024),
        name="step",
    )(info, images, *parts, head)


def rotate(k):
    return [(i, (i + k) % 4) for i in range(4)]


def along(axis, k):
    if axis == "x":
        return "segment", rotate(k)
    pairs = []
    for d in range(32):
        y, z, c = d // 8, d // 2 % 4, d % 2
        if axis == "y":
            y = (y + k) % 4
        elif axis == "z":
            z = (z + k) % 4
        else:
            c = c ^ 1
        pairs.append((d, y * 8 + z * 2 + c))
    return "dp", pairs


def move(value, axis, k=1):
    name, pairs = along(axis, k)
    return lax.ppermute(value, name, pairs)


def reduce_ring(value, axis):
    return value[0] + move(value[1], axis, 1) + move(value[2], axis, 2) + move(value[3], axis, 3)


def local(images, labels, counts, depthwise, pointwise, head_weight):
    seg = lax.axis_index("segment")
    dp = lax.axis_index("dp")
    my_y, my_z, core = dp // 8, dp // 2 % 4, dp % 2
    info = jnp.stack([counts[0], counts[1], counts[2], counts[3], seg, core, my_y, my_z,
                      lax.dynamic_index_in_dim(labels, seg, 0, keepdims=False)]).astype(jnp.int32)
    own = jnp.concatenate([pointwise, jnp.pad(depthwise, ((0, 0), (0, 7), (0, 0)))], axis=1)
    half = lax.dynamic_slice_in_dim(own, 2 * core, 2, 0)
    near = [move(half, "x", k) for k in (1, 2, 3)]
    far = [move(part, "core") for part in near]
    out0, out1 = run_step(info, images.reshape(4, POS, CHAN), [own, *near, *far], head_weight)
    out0 = out0[0] + move(out0[1], "core")
    out1 = out1[0] + move(out1[1], "core")
    out0 = reduce_ring(reduce_ring(out0, "y"), "z")
    out1 = reduce_ring(reduce_ring(out1, "z"), "y")
    taps = jnp.transpose(out0[ROWS:].reshape(16, 4, LANE), (1, 0, 2))
    slots = jnp.stack([out0[:ROWS].reshape(4, 2, 16, CHAN), out1.reshape(4, 2, 16, CHAN)], axis=2)
    slots = slots.reshape(4, 64, CHAN)
    payload = jnp.concatenate([slots, jnp.pad(taps, ((0, 0), (0, 0), (0, CHAN - LANE)))], axis=1)
    pieces = [lax.dynamic_index_in_dim(payload, (seg + k) % 4, 0, keepdims=False) for k in range(4)]
    final = pieces[0] + move(pieces[1], "x", 1) + move(pieces[2], "x", 2) + move(pieces[3], "x", 3)
    grad_pointwise = final[:64].reshape(4, 16, CHAN)
    grad_taps = final[64:, :64].reshape(16, 4, 16)[:, :, :9]
    return grad_pointwise, jnp.transpose(grad_taps, (1, 2, 0))


def solution(mesh):
    in_specs = (P("dp", None, None, None), P("dp"), P(), P("segment", None, None), P("segment", None, None), P())
    out_specs = (P("segment", "dp", None), P("segment", None, "dp"))
    return jax.shard_map(local, mesh=mesh, in_specs=in_specs, out_specs=out_specs, check_vma=False)
```

```python
import jax
import jax.numpy as jnp
from jax import lax
from jax.experimental import pallas as pl
from jax.experimental.pallas import tpu as pltpu
from jax.sharding import PartitionSpec as P

F32 = jnp.float32
BF16 = jnp.bfloat16
SIDE, POS, CHAN, LANE, CLASSES = 16, 256, 512, 128, 1000
TAPS = [(a, b) for a in (-1, 0, 1) for b in (-1, 0, 1)]
COLOR_ROWS = (80, 80, 64)


def step_kernel(counts, labels, images, own, *rest):
    tap_parts, rest = (rest[:4], rest[4:])
    near, far = (rest[0:8], rest[8:16])
    head = rest[16]
    keeps, sends = (rest[17:20], rest[20:23])
    (wv, dv, xs, us, pad, dyb, gw, zero, gds, gdt, hv, wsem, dsem, isem, hsem, gsem, zsem, tsem) = rest[23:]
    seg, dp = (lax.axis_index("segment"), lax.axis_index("dp"))
    core, my_y, my_z = (lax.rem(dp, 2), dp // 8, lax.rem(dp // 2, 4))
    image_copy = pltpu.make_async_copy(images.at[seg], xs.at[0], isem)
    image_copy.start()
    tap_copies = [pltpu.make_async_copy(part, dv.at[lax.rem(seg - k + 4, 4)], dsem.at[k])
                  for k, part in enumerate(tap_parts)]
    for copy in tap_copies:
        copy.start()

    def fetch(section, carry):
        @pl.when(section == seg)
        def _():
            pltpu.make_async_copy(own, wv.at[seg], wsem.at[seg]).start()

        @pl.when(section != seg)
        def _():
            r = lax.rem(seg - section + 4, 4) - 1
            for half, mine in ((0, my_z), (1, my_y)):
                for k in range(4):
                    row = pl.multiple_of(lax.rem(mine - k + 4, 4) * 128, 128)
                    pltpu.make_async_copy(near[4 * half + k].at[r],
                                          wv.at[section, 2 * half + core, pl.ds(row, 128)], wsem.at[section]).start()
                    pltpu.make_async_copy(far[4 * half + k].at[r],
                                          wv.at[section, 2 * half + 1 - core, pl.ds(row, 128)], wsem.at[section]).start()
        return carry

    lax.fori_loop(0, 4, fetch, 0)
    head_copy = pltpu.make_async_copy(head, hv, hsem)
    head_copy.start()
    pad[...] = jnp.zeros(pad.shape, F32)
    gds[...] = jnp.zeros(gds.shape, F32)
    zero[...] = jnp.zeros(zero.shape, F32)
    total = counts[0] + counts[1] + counts[2] + counts[3]

    def push(buf, m, sem):
        q = jnp.where(m >= 5, 1, 0) + jnp.where(m >= 10, 1, 0)
        row = pl.multiple_of((m - 5 * q) * 16, 16)
        for color in range(3):
            @pl.when(q == color)
            def _():
                for side, outs in enumerate((keeps, sends)):
                    for xb in range(4):
                        pltpu.make_async_copy(
                            buf.at[:, jnp.bitwise_xor(core, side), :, xb * LANE:xb * LANE + LANE],
                            outs[color].at[:, xb, pl.ds(row, 16)], sem).start()

    for m in range(7, 13):
        @pl.when(m >= total)
        def _():
            push(zero, m, zsem.at[m - 7])
    image_copy.wait()
    for copy in tap_copies:
        copy.wait()

    def live_base(section):
        base = jnp.int32(0)
        for s in range(3):
            base = base + jnp.where(s < section, counts[s], 0)
        return base

    def lanes(cb):
        return pl.ds(pl.multiple_of(cb * LANE, LANE), LANE)

    def forward_cell(section, slot, n, dil):
        def block(cb, carry):
            field = xs[n, :, lanes(cb)].astype(F32)
            pad[cb, 2:18, 8:24, :] = jnp.maximum(field, 0.0).reshape(SIDE, SIDE, LANE)
            taps = dv[section, slot, :, lanes(cb)].astype(F32)
            for rb in range(4):
                mixed = jnp.zeros((4, SIDE, LANE), F32)
                for t, (a, b) in enumerate(TAPS):
                    view = pad[cb, 2 + 4 * rb + a * dil:6 + 4 * rb + a * dil, 8 + b * dil:24 + b * dil, :]
                    mixed = mixed + view * taps[t]
                us[n, 64 * rb:64 * rb + 64, lanes(cb)] = mixed.reshape(64, LANE).astype(BF16)
            return carry
        lax.fori_loop(0, 4, block, 0)
        y = jnp.dot(us[n], wv[section, slot], preferred_element_type=F32)
        xs[n + 1] = (xs[n].astype(F32) + y).astype(BF16)

    def forward_pair(p, carry):
        section = p // 2
        base = live_base(section)

        @pl.when(lax.rem(p, 2) == 0)
        def _():
            pltpu.make_async_copy(wv.at[section], wv.at[section], wsem.at[section]).wait()
        for par in range(2):
            slot = 2 * lax.rem(p, 2) + par

            @pl.when(slot < counts[section])
            def _():
                forward_cell(section, slot, base + slot, 1 + par)
        return carry

    lax.fori_loop(0, 8, forward_pair, 0)

    head_copy.wait()
    final = xs[total].astype(F32)
    pooled = jnp.sum(final, axis=0, keepdims=True) / POS
    logits = jnp.sum(hv[...] * pooled, axis=1, keepdims=True)
    classes = lax.broadcasted_iota(jnp.int32, (CLASSES, 1), 0)
    target = jnp.where(classes == labels[seg], 1.0, 0.0)
    err = (jax.nn.sigmoid(logits) - target) / 128
    back = jnp.sum(hv[...] * err, axis=0, keepdims=True) / POS
    dyb[...] = jnp.broadcast_to(back, (POS, CHAN)).astype(BF16)

    def backward_cell(section, slot, n, m, dil, par):
        dy = dyb[...]
        grad = lax.dot_general(us[n], dy, (((0,), (0,)), ((), ())), preferred_element_type=F32)
        gw[par] = grad.reshape(16, 2, 16, CHAN)
        du = lax.dot_general(dy, wv[section, slot], (((1,), (1,)), ((), ())), preferred_element_type=F32)
        du = du.astype(BF16).astype(F32)
        for cb in range(4):
            pad[cb, 2:18, 8:24, :] = du[:, cb * LANE:cb * LANE + LANE].reshape(SIDE, SIDE, LANE)

        def block(cb, carry):
            taps = dv[section, slot, :, lanes(cb)].astype(F32)
            sums = [jnp.zeros((SIDE, LANE), F32) for _ in TAPS]
            for rb in range(4):
                x = xs[n, 64 * rb:64 * rb + 64, lanes(cb)].astype(F32)
                r = jnp.maximum(x, 0.0).reshape(4, SIDE, LANE)
                acc = jnp.zeros((4, SIDE, LANE), F32)
                for t, (a, b) in enumerate(TAPS):
                    view = pad[cb, 2 + 4 * rb - a * dil:6 + 4 * rb - a * dil, 8 - b * dil:24 - b * dil, :]
                    acc = acc + view * taps[t]
                    sums[t] = sums[t] + jnp.sum(view * r, axis=0)
                old = dyb[64 * rb:64 * rb + 64, lanes(cb)].astype(F32)
                dyb[64 * rb:64 * rb + 64, lanes(cb)] = (
                    old + jnp.where(x > 0, acc.reshape(64, LANE), 0.0)).astype(BF16)
            rows = [jnp.sum(v, axis=0, keepdims=True) for v in sums]
            rows.append(jnp.zeros((7, LANE), F32))
            gds[m, :, lanes(cb)] = jnp.concatenate(rows, axis=0)
            return carry
        lax.fori_loop(0, 4, block, 0)

    def drain(par):
        pltpu.make_async_copy(gw.at[par], gw.at[par], gsem.at[par]).wait()

    def backward_pair(q, used):
        p = 7 - q
        section = p // 2
        base = live_base(section)
        used = list(used)
        for par in (1, 0):
            slot = 2 * lax.rem(p, 2) + par
            live = slot < counts[section]
            m = total - 1 - base - slot

            @pl.when(jnp.logical_and(live, used[par] > 0))
            def _():
                drain(par)

            @pl.when(live)
            def _():
                backward_cell(section, slot, base + slot, m, 1 + par, par)
                push(gw.at[par], m, gsem.at[par])
            used[par] = jnp.where(live, 1, used[par])
        return tuple(used)

    used = lax.fori_loop(0, 8, backward_pair, (jnp.int32(0), jnp.int32(0)))
    flat = jnp.concatenate([gds[m, 0:9, :] for m in range(13)] + [jnp.zeros((11, CHAN), F32)], axis=0)
    gdt[...] = jnp.transpose(flat).reshape(16, 2, 16, LANE)
    tails = []
    for side, outs in enumerate((keeps, sends)):
        for xb in range(4):
            block = (gdt.at[:, jnp.bitwise_xor(core, side)] if xb == 0
                     else zero.at[:, jnp.bitwise_xor(core, side), :, 0:LANE])
            tails.append(pltpu.make_async_copy(block, outs[2].at[:, xb, pl.ds(48, 16)], tsem.at[side, xb]))
    for copy in tails:
        copy.start()
    for par in range(2):
        @pl.when(used[par] > 0)
        def _():
            drain(par)
    for m in range(7, 13):
        @pl.when(m >= total)
        def _():
            pltpu.make_async_copy(zero, zero, zsem.at[m - 7]).wait()
    for copy in tails:
        copy.wait()


def run_step(counts, labels, images, own, taps, near, far, head):
    hbm = pl.BlockSpec(memory_space=pl.ANY)
    smem = pl.BlockSpec(memory_space=pltpu.SMEM)
    shapes = [jax.ShapeDtypeStruct((16, 4, rows, LANE), F32) for rows in COLOR_ROWS]
    return pl.pallas_call(
        step_kernel,
        in_specs=[smem, smem] + [hbm] * 23,
        out_specs=[hbm] * 6,
        out_shape=shapes + shapes,
        scratch_shapes=[
            pltpu.VMEM((4, 4, CHAN, CHAN), BF16),
            pltpu.VMEM((4, 4, 16, CHAN), BF16),
            pltpu.VMEM((14, POS, CHAN), BF16),
            pltpu.VMEM((13, POS, CHAN), BF16),
            pltpu.VMEM((4, 20, 32, LANE), F32),
            pltpu.VMEM((POS, CHAN), BF16),
            pltpu.VMEM((2, 16, 2, 16, CHAN), F32),
            pltpu.VMEM((16, 2, 16, CHAN), F32),
            pltpu.VMEM((13, 16, CHAN), F32),
            pltpu.VMEM((16, 2, 16, LANE), F32),
            pltpu.VMEM((CLASSES, CHAN), F32),
            pltpu.SemaphoreType.DMA((4,)),
            pltpu.SemaphoreType.DMA((4,)),
            pltpu.SemaphoreType.DMA,
            pltpu.SemaphoreType.DMA,
            pltpu.SemaphoreType.DMA((2,)),
            pltpu.SemaphoreType.DMA((6,)),
            pltpu.SemaphoreType.DMA((2, 4)),
        ],
        compiler_params=pltpu.CompilerParams(vmem_limit_bytes=56 * 1024 * 1024),
        name="step",
    )(counts, labels, images, own, *taps, *near, *far, head)


def finish_kernel(counts, r0, r1, r2, r3, grad_pointwise, grad_depthwise, turned):
    seg = lax.axis_index("segment")
    total = counts[0] + counts[1] + counts[2] + counts[3]
    base = jnp.int32(0)
    for s in range(3):
        base = base + jnp.where(s < seg, counts[s], 0)
    here = counts[seg]
    taps = jnp.zeros((16, LANE), F32)
    for k, part in enumerate((r0, r1, r2, r3)):
        lane = pl.multiple_of(lax.rem(seg - k + 4, 4) * LANE, LANE)
        for j in range(4):
            rows = part[48 - 16 * j:64 - 16 * j, :]
            grad_pointwise[j, :, pl.ds(lane, LANE)] = jnp.where(j < here, rows, 0.0)
        taps = taps + part[64:80, :]
    turned[...] = jnp.transpose(taps)
    for j in range(4):
        first = jnp.maximum(total - 1 - base - j, 0) * 9
        grad_depthwise[j] = jnp.where(j < here, turned[pl.ds(first, 9), :], 0.0)


def finish(counts, parts):
    vmem = pl.BlockSpec(memory_space=pltpu.VMEM)
    return pl.pallas_call(
        finish_kernel,
        in_specs=[pl.BlockSpec(memory_space=pltpu.SMEM)] + [vmem] * 4,
        out_specs=[vmem, vmem],
        out_shape=[jax.ShapeDtypeStruct((4, 16, CHAN), F32), jax.ShapeDtypeStruct((4, 9, 16), F32)],
        scratch_shapes=[pltpu.VMEM((LANE, 16), F32)],
        name="finish",
    )(counts, *parts)


def rotate(k):
    return [(i, (i + k) % 4) for i in range(4)]


def along(axis, k):
    if axis == "x":
        return "segment", rotate(k)
    pairs = []
    for d in range(32):
        y, z, c = d // 8, d // 2 % 4, d % 2
        if axis == "y":
            y = (y + k) % 4
        elif axis == "z":
            z = (z + k) % 4
        else:
            c = c ^ 1
        pairs.append((d, y * 8 + z * 2 + c))
    return "dp", pairs


def move(value, axis, k=1):
    name, pairs = along(axis, k)
    return lax.ppermute(value, name, pairs)


def gather_weights(pointwise, depthwise, place):
    core, my_y, my_z = place["core"], place["y"], place["z"]
    taps = jnp.pad(depthwise, ((0, 0), (0, 7), (0, 0)))
    first = lax.dynamic_slice(pointwise, (core, my_z * 128, 0), (1, 128, CHAN))
    second = lax.dynamic_slice(pointwise, (2 + core, my_y * 128, 0), (1, 128, CHAN))
    piece = jnp.concatenate([first, second], axis=0)
    pieces = [move(piece, "x", k) for k in (1, 2, 3)]
    all_taps = [taps] + [move(taps, "x", k) for k in (1, 2, 3)]
    near = []
    for half, axis in ((0, "z"), (1, "y")):
        mine = jnp.stack([p[half] for p in pieces])
        near += [mine] + [move(mine, axis, k) for k in (1, 2, 3)]
    far = [move(part, "core") for part in near]
    return near, far, all_taps


def reduce_color(keep, send, axes, place):
    rows = keep.shape[2]
    value = (keep + move(send, "core")).reshape(4, 4, 4, rows, LANE)
    names = ["y", "z", "x"]
    for axis in axes:
        dim = names.index(axis)
        names.pop(dim)
        pieces = [lax.dynamic_index_in_dim(value, (place[axis] + k) % 4, dim, keepdims=False) for k in range(4)]
        value = pieces[0]
        for k in (1, 3, 2):
            value = value + move(pieces[k], axis, k)
    return value


def local(images, labels, counts, depthwise, pointwise, head_weight):
    seg = lax.axis_index("segment")
    dp = lax.axis_index("dp")
    place = {"x": seg, "y": dp // 8, "z": dp // 2 % 4, "core": dp % 2}
    near, far, taps = gather_weights(pointwise, depthwise, place)
    outs = run_step(counts, labels, images.reshape(4, POS, CHAN), pointwise, taps, near, far, head_weight.T)
    sums = [reduce_color(outs[q], outs[3 + q], axes, place) for q, axes in enumerate(("xyz", "yzx", "zxy"))]
    ordered = jnp.concatenate([jnp.zeros((48, LANE), F32), *sums], axis=0)
    total = jnp.sum(counts)
    before = jnp.cumsum(counts) - counts
    taps_rows = ordered[256:272]
    parts = []
    for k in range(4):
        dest = (seg + k) % 4
        start = (total - 1 - lax.dynamic_index_in_dim(before, dest, 0, keepdims=False)) * 16
        piece = jnp.concatenate([lax.dynamic_slice_in_dim(ordered, start, 64, 0), taps_rows], axis=0)
        parts.append(move(piece, "x", k) if k else piece)
    grad_pointwise, grad_depthwise = finish(counts, parts)
    return grad_pointwise, grad_depthwise


def solution(mesh):
    in_specs = (P("dp", None, None, None), P("dp"), P(), P("segment", None, None), P("segment", None, None), P())
    out_specs = (P("segment", "dp", None), P("segment", None, "dp"))
    return jax.shard_map(local, mesh=mesh, in_specs=in_specs, out_specs=out_specs, check_vma=False)
```

```python
import jax
import jax.numpy as jnp
from jax import lax
from jax.experimental import pallas as pl
from jax.experimental.pallas import tpu as pltpu
from jax.sharding import PartitionSpec as P

F32 = jnp.float32
BF16 = jnp.bfloat16
SIDE, POS, CHAN, LANE, CLASSES = 16, 256, 512, 128, 1000
TAPS = [(a, b) for a in (-1, 0, 1) for b in (-1, 0, 1)]
COLOR_ROWS = (80, 80, 64)


def step_kernel(counts, labels, images, own, *rest):
    own_taps, pieces, swapped = (rest[0], rest[1:4], rest[4])
    near, far = (rest[5:11], rest[11:17])
    head, rest = (rest[17], rest[1:])
    keeps, sends = (rest[17:20], rest[20:23])
    (wv, dv, xs, us, pad, dyb, gw, zero, gds, gdt, hv, wsem, dsem, isem, hsem, gsem, zsem, tsem) = rest[23:]
    seg, dp = (lax.axis_index("segment"), lax.axis_index("dp"))
    core, my_y, my_z = (lax.rem(dp, 2), dp // 8, lax.rem(dp // 2, 4))
    image_copy = pltpu.make_async_copy(images.at[seg], xs.at[0], isem)
    image_copy.start()
    tap_copies = [pltpu.make_async_copy(own_taps, dv.at[seg], dsem.at[0])]
    for k, piece in enumerate(pieces, 1):
        tap_copies.append(pltpu.make_async_copy(piece.at[pl.ds(256, 64)].reshape(4, 16, CHAN),
                                                dv.at[lax.rem(seg - k + 4, 4)], dsem.at[k]))
    for copy in tap_copies:
        copy.start()

    def fetch(section, carry):
        @pl.when(section == seg)
        def _():
            pltpu.make_async_copy(own, wv.at[seg], wsem.at[seg]).start()

        @pl.when(section != seg)
        def _():
            r = lax.rem(seg - section + 4, 4) - 1
            for half, mine in ((0, my_z), (1, my_y)):
                def place(part, slot, k):
                    row = pl.multiple_of(lax.rem(mine - k + 4, 4) * 128, 128)
                    pltpu.make_async_copy(part, wv.at[section, slot, pl.ds(row, 128)], wsem.at[section]).start()

                for turn, piece in enumerate(pieces):
                    @pl.when(r == turn)
                    def _():
                        place(piece.at[pl.ds(128 * half, 128)], 2 * half + core, 0)
                place(swapped.at[half, r], 2 * half + 1 - core, 0)
                for k in range(1, 4):
                    place(near[3 * half + k - 1].at[r], 2 * half + core, k)
                    place(far[3 * half + k - 1].at[r], 2 * half + 1 - core, k)
        return carry

    lax.fori_loop(0, 4, fetch, 0)
    head_copy = pltpu.make_async_copy(head, hv, hsem)
    head_copy.start()
    pad[...] = jnp.zeros(pad.shape, F32)
    gds[...] = jnp.zeros(gds.shape, F32)
    zero[...] = jnp.zeros(zero.shape, F32)
    total = counts[0] + counts[1] + counts[2] + counts[3]

    def push(buf, m, sem):
        q = jnp.where(m >= 5, 1, 0) + jnp.where(m >= 10, 1, 0)
        row = pl.multiple_of((m - 5 * q) * 16, 16)
        for color in range(3):
            @pl.when(q == color)
            def _():
                for side, outs in enumerate((keeps, sends)):
                    for xb in range(4):
                        pltpu.make_async_copy(
                            buf.at[:, jnp.bitwise_xor(core, side), :, xb * LANE:xb * LANE + LANE],
                            outs[color].at[:, xb, pl.ds(row, 16)], sem).start()

    for m in range(7, 13):
        @pl.when(m >= total)
        def _():
            push(zero, m, zsem.at[m - 7])
    image_copy.wait()
    for copy in tap_copies:
        copy.wait()

    def live_base(section):
        base = jnp.int32(0)
        for s in range(3):
            base = base + jnp.where(s < section, counts[s], 0)
        return base

    def lanes(cb):
        return pl.ds(pl.multiple_of(cb * LANE, LANE), LANE)

    def forward_cell(section, slot, n, dil):
        def block(cb, carry):
            field = xs[n, :, lanes(cb)].astype(F32)
            pad[cb, 2:18, 8:24, :] = jnp.maximum(field, 0.0).reshape(SIDE, SIDE, LANE)
            taps = dv[section, slot, :, lanes(cb)].astype(F32)
            for rb in range(4):
                mixed = jnp.zeros((4, SIDE, LANE), F32)
                for t, (a, b) in enumerate(TAPS):
                    view = pad[cb, 2 + 4 * rb + a * dil:6 + 4 * rb + a * dil, 8 + b * dil:24 + b * dil, :]
                    mixed = mixed + view * taps[t]
                us[n, 64 * rb:64 * rb + 64, lanes(cb)] = mixed.reshape(64, LANE).astype(BF16)
            return carry
        lax.fori_loop(0, 4, block, 0)
        y = jnp.dot(us[n], wv[section, slot], preferred_element_type=F32)
        xs[n + 1] = (xs[n].astype(F32) + y).astype(BF16)

    def forward_pair(p, carry):
        section = p // 2
        base = live_base(section)

        @pl.when(lax.rem(p, 2) == 0)
        def _():
            pltpu.make_async_copy(wv.at[section], wv.at[section], wsem.at[section]).wait()
        for par in range(2):
            slot = 2 * lax.rem(p, 2) + par

            @pl.when(slot < counts[section])
            def _():
                forward_cell(section, slot, base + slot, 1 + par)
        return carry

    lax.fori_loop(0, 8, forward_pair, 0)

    head_copy.wait()
    final = xs[total].astype(F32)
    pooled = jnp.sum(final, axis=0, keepdims=True) / POS
    logits = jnp.sum(hv[...] * pooled, axis=1, keepdims=True)
    classes = lax.broadcasted_iota(jnp.int32, (CLASSES, 1), 0)
    target = jnp.where(classes == labels[seg], 1.0, 0.0)
    err = (jax.nn.sigmoid(logits) - target) / 128
    back = jnp.sum(hv[...] * err, axis=0, keepdims=True) / POS
    dyb[...] = jnp.broadcast_to(back, (POS, CHAN)).astype(BF16)

    def backward_cell(section, slot, n, m, dil, par):
        dy = dyb[...]
        grad = lax.dot_general(us[n], dy, (((0,), (0,)), ((), ())), preferred_element_type=F32)
        gw[par] = grad.reshape(16, 2, 16, CHAN)
        du = lax.dot_general(dy, wv[section, slot], (((1,), (1,)), ((), ())), preferred_element_type=F32)
        du = du.astype(BF16).astype(F32)
        for cb in range(4):
            pad[cb, 2:18, 8:24, :] = du[:, cb * LANE:cb * LANE + LANE].reshape(SIDE, SIDE, LANE)

        def block(cb, carry):
            taps = dv[section, slot, :, lanes(cb)].astype(F32)
            sums = [jnp.zeros((SIDE, LANE), F32) for _ in TAPS]
            for rb in range(4):
                x = xs[n, 64 * rb:64 * rb + 64, lanes(cb)].astype(F32)
                r = jnp.maximum(x, 0.0).reshape(4, SIDE, LANE)
                acc = jnp.zeros((4, SIDE, LANE), F32)
                for t, (a, b) in enumerate(TAPS):
                    view = pad[cb, 2 + 4 * rb - a * dil:6 + 4 * rb - a * dil, 8 - b * dil:24 - b * dil, :]
                    acc = acc + view * taps[t]
                    sums[t] = sums[t] + jnp.sum(view * r, axis=0)
                old = dyb[64 * rb:64 * rb + 64, lanes(cb)].astype(F32)
                dyb[64 * rb:64 * rb + 64, lanes(cb)] = (
                    old + jnp.where(x > 0, acc.reshape(64, LANE), 0.0)).astype(BF16)
            rows = [jnp.sum(v, axis=0, keepdims=True) for v in sums]
            rows.append(jnp.zeros((7, LANE), F32))
            gds[m, :, lanes(cb)] = jnp.concatenate(rows, axis=0)
            return carry
        lax.fori_loop(0, 4, block, 0)

    def drain(par):
        pltpu.make_async_copy(gw.at[par], gw.at[par], gsem.at[par]).wait()

    def backward_pair(q, used):
        p = 7 - q
        section = p // 2
        base = live_base(section)
        used = list(used)
        for par in (1, 0):
            slot = 2 * lax.rem(p, 2) + par
            live = slot < counts[section]
            m = total - 1 - base - slot

            @pl.when(jnp.logical_and(live, used[par] > 0))
            def _():
                drain(par)

            @pl.when(live)
            def _():
                backward_cell(section, slot, base + slot, m, 1 + par, par)
                push(gw.at[par], m, gsem.at[par])
            used[par] = jnp.where(live, 1, used[par])
        return tuple(used)

    used = lax.fori_loop(0, 8, backward_pair, (jnp.int32(0), jnp.int32(0)))
    flat = jnp.concatenate([gds[m, 0:9, :] for m in range(13)] + [jnp.zeros((11, CHAN), F32)], axis=0)
    gdt[...] = jnp.transpose(flat).reshape(16, 2, 16, LANE)
    tails = []
    for side, outs in enumerate((keeps, sends)):
        for xb in range(4):
            block = (gdt.at[:, jnp.bitwise_xor(core, side)] if xb == 0
                     else zero.at[:, jnp.bitwise_xor(core, side), :, 0:LANE])
            tails.append(pltpu.make_async_copy(block, outs[2].at[:, xb, pl.ds(48, 16)], tsem.at[side, xb]))
    for copy in tails:
        copy.start()
    for par in range(2):
        @pl.when(used[par] > 0)
        def _():
            drain(par)
    for m in range(7, 13):
        @pl.when(m >= total)
        def _():
            pltpu.make_async_copy(zero, zero, zsem.at[m - 7]).wait()
    for copy in tails:
        copy.wait()


def run_step(counts, labels, images, own, weights, head):
    hbm = pl.BlockSpec(memory_space=pl.ANY)
    smem = pl.BlockSpec(memory_space=pltpu.SMEM)
    shapes = [jax.ShapeDtypeStruct((16, 4, rows, LANE), F32) for rows in COLOR_ROWS]
    return pl.pallas_call(
        step_kernel,
        in_specs=[smem, smem] + [hbm] * 20,
        out_specs=[hbm] * 6,
        out_shape=shapes + shapes,
        scratch_shapes=[
            pltpu.VMEM((4, 4, CHAN, CHAN), BF16),
            pltpu.VMEM((4, 4, 16, CHAN), BF16),
            pltpu.VMEM((14, POS, CHAN), BF16),
            pltpu.VMEM((13, POS, CHAN), BF16),
            pltpu.VMEM((4, 20, 32, LANE), F32),
            pltpu.VMEM((POS, CHAN), BF16),
            pltpu.VMEM((2, 16, 2, 16, CHAN), F32),
            pltpu.VMEM((16, 2, 16, CHAN), F32),
            pltpu.VMEM((13, 16, CHAN), F32),
            pltpu.VMEM((16, 2, 16, LANE), F32),
            pltpu.VMEM((CLASSES, CHAN), F32),
            pltpu.SemaphoreType.DMA((4,)),
            pltpu.SemaphoreType.DMA((4,)),
            pltpu.SemaphoreType.DMA,
            pltpu.SemaphoreType.DMA,
            pltpu.SemaphoreType.DMA((2,)),
            pltpu.SemaphoreType.DMA((6,)),
            pltpu.SemaphoreType.DMA((2, 4)),
        ],
        compiler_params=pltpu.CompilerParams(vmem_limit_bytes=56 * 1024 * 1024),
        name="step",
    )(counts, labels, images, own, *weights, head)


def finish_kernel(counts, r0, r1, r2, r3, grad_pointwise, grad_depthwise, turned):
    seg = lax.axis_index("segment")
    total = counts[0] + counts[1] + counts[2] + counts[3]
    base = jnp.int32(0)
    for s in range(3):
        base = base + jnp.where(s < seg, counts[s], 0)
    here = counts[seg]
    taps = jnp.zeros((16, LANE), F32)
    for k, part in enumerate((r0, r1, r2, r3)):
        lane = pl.multiple_of(lax.rem(seg - k + 4, 4) * LANE, LANE)
        for j in range(4):
            rows = part[48 - 16 * j:64 - 16 * j, :]
            grad_pointwise[j, :, pl.ds(lane, LANE)] = jnp.where(j < here, rows, 0.0)
        taps = taps + part[64:80, :]
    turned[...] = jnp.transpose(taps)
    for j in range(4):
        first = jnp.maximum(total - 1 - base - j, 0) * 9
        grad_depthwise[j] = jnp.where(j < here, turned[pl.ds(first, 9), :], 0.0)


def finish(counts, parts):
    vmem = pl.BlockSpec(memory_space=pltpu.VMEM)
    return pl.pallas_call(
        finish_kernel,
        in_specs=[pl.BlockSpec(memory_space=pltpu.SMEM)] + [vmem] * 4,
        out_specs=[vmem, vmem],
        out_shape=[jax.ShapeDtypeStruct((4, 16, CHAN), F32), jax.ShapeDtypeStruct((4, 9, 16), F32)],
        scratch_shapes=[pltpu.VMEM((LANE, 16), F32)],
        name="finish",
    )(counts, *parts)


def rotate(k):
    return [(i, (i + k) % 4) for i in range(4)]


def along(axis, k):
    if axis == "x":
        return "segment", rotate(k)
    pairs = []
    for d in range(32):
        y, z, c = d // 8, d // 2 % 4, d % 2
        if axis == "y":
            y = (y + k) % 4
        elif axis == "z":
            z = (z + k) % 4
        else:
            c = c ^ 1
        pairs.append((d, y * 8 + z * 2 + c))
    return "dp", pairs


def move(value, axis, k=1):
    name, pairs = along(axis, k)
    return lax.ppermute(value, name, pairs)


def gather_weights(pointwise, depthwise, place):
    core, my_y, my_z = place["core"], place["y"], place["z"]
    taps = jnp.pad(depthwise, ((0, 0), (0, 7), (0, 0)))
    first = lax.dynamic_slice(pointwise, (core, my_z * 128, 0), (1, 128, CHAN))
    second = lax.dynamic_slice(pointwise, (2 + core, my_y * 128, 0), (1, 128, CHAN))
    piece = jnp.concatenate([first[0], second[0], taps.reshape(64, CHAN)], axis=0)
    pieces = [move(piece, "x", k) for k in (1, 2, 3)]
    pieces = lax.optimization_barrier(pieces)
    halves = [jnp.stack([p[128 * half:128 * half + 128] for p in pieces]) for half in (0, 1)]
    halves = lax.optimization_barrier(halves)
    near = [move(halves[half], axis, k) for half, axis in ((0, "z"), (1, "y")) for k in (1, 3, 2)]
    near = near[0:1] + near[2:3] + near[1:2] + near[3:4] + near[5:6] + near[4:5]
    swapped = move(jnp.stack(halves), "core")
    far = [move(part, "core") for part in near]
    return [taps, *pieces, swapped, *near, *far]


def reduce_colors(keeps, sends, orders, place):
    values = [keep + move(send, "core") for keep, send in zip(keeps, sends)]
    values = [value.reshape(4, 4, 4, *value.shape[2:]) for value in values]
    names = [["y", "z", "x"] for _ in values]
    for stage in range(3):
        values = lax.optimization_barrier(values)
        pieces = []
        for q, value in enumerate(values):
            axis = orders[q][stage]
            dim = names[q].index(axis)
            names[q].pop(dim)
            pieces.append([lax.dynamic_index_in_dim(value, (place[axis] + k) % 4, dim, keepdims=False)
                           for k in range(4)])
        pieces = lax.optimization_barrier(pieces)
        moved = [[pieces[q][0]] for q in range(3)]
        for k in (1, 3, 2):
            for q in range(3):
                moved[q].append(move(pieces[q][k], orders[q][stage], k))
        moved = lax.optimization_barrier(moved)
        values = [m[0] + m[1] + m[2] + m[3] for m in moved]
    return values


def local(images, labels, counts, depthwise, pointwise, head_weight):
    seg = lax.axis_index("segment")
    dp = lax.axis_index("dp")
    place = {"x": seg, "y": dp // 8, "z": dp // 2 % 4, "core": dp % 2}
    weights = gather_weights(pointwise, depthwise, place)
    outs = run_step(counts, labels, images.reshape(4, POS, CHAN), pointwise, weights, head_weight.T)
    sums = reduce_colors(outs[:3], outs[3:], ("xyz", "yzx", "zxy"), place)
    ordered = jnp.concatenate([jnp.zeros((48, LANE), F32), *sums], axis=0)
    total = jnp.sum(counts)
    before = jnp.cumsum(counts) - counts
    taps_rows = ordered[256:272]
    parts = []
    for k in range(4):
        dest = (seg + k) % 4
        start = (total - 1 - lax.dynamic_index_in_dim(before, dest, 0, keepdims=False)) * 16
        piece = jnp.concatenate([lax.dynamic_slice_in_dim(ordered, start, 64, 0), taps_rows], axis=0)
        parts.append(move(piece, "x", k) if k else piece)
    grad_pointwise, grad_depthwise = finish(counts, parts)
    return grad_pointwise, grad_depthwise


def solution(mesh):
    in_specs = (P("dp", None, None, None), P("dp"), P(), P("segment", None, None), P("segment", None, None), P())
    out_specs = (P("segment", "dp", None), P("segment", None, "dp"))
    return jax.shard_map(local, mesh=mesh, in_specs=in_specs, out_specs=out_specs, check_vma=False)
```

```python
import jax
import jax.numpy as jnp
from jax import lax
from jax.experimental import pallas as pl
from jax.experimental.pallas import tpu as pltpu
from jax.sharding import PartitionSpec as P

F32 = jnp.float32
BF16 = jnp.bfloat16
SIDE, POS, CHAN, LANE, CLASSES = 16, 256, 512, 128, 1000
TAPS = [(a, b) for a in (-1, 0, 1) for b in (-1, 0, 1)]
HALF_ROWS = 112


def step_kernel(counts, labels, images, own, *rest):
    own_taps, pieces, whole, other = (rest[0], rest[1:4], rest[4:7], rest[7:10])
    swapped, near, far, head = (rest[10], rest[11:14], rest[14:17], rest[17])
    keeps, sends, rest = (rest[18:20], rest[20:22], rest[22:])
    (wv, dv, xs, us, pad, dyb, gw, zero, gds, gdt, hv, wsem, dsem, isem, hsem, gsem, zsem, tsem) = rest
    seg, dp = (lax.axis_index("segment"), lax.axis_index("dp"))
    core, my_z = (lax.rem(dp, 2), lax.rem(dp // 2, 4))
    image_copy = pltpu.make_async_copy(images.at[seg], xs.at[0], isem)
    image_copy.start()
    tap_copies = [pltpu.make_async_copy(own_taps, dv.at[seg], dsem.at[0])]
    for k, piece in enumerate(pieces, 1):
        tap_copies.append(pltpu.make_async_copy(piece.at[pl.ds(128, 64)].reshape(4, 16, CHAN),
                                                dv.at[lax.rem(seg - k + 4, 4)], dsem.at[k]))
    for copy in tap_copies:
        copy.start()

    def fetch(section, carry):
        @pl.when(section == seg)
        def _():
            pltpu.make_async_copy(own, wv.at[seg], wsem.at[seg]).start()

        @pl.when(section != seg)
        def _():
            r = lax.rem(seg - section + 4, 4) - 1

            def place(part, slot, k):
                row = pl.multiple_of(lax.rem(my_z - k + 4, 4) * 128, 128)
                pltpu.make_async_copy(part, wv.at[section, slot, pl.ds(row, 128)], wsem.at[section]).start()

            for turn in range(3):
                @pl.when(r == turn)
                def _():
                    place(pieces[turn].at[pl.ds(0, 128)], 2 + core, 0)
                    pltpu.make_async_copy(whole[turn], wv.at[section, core], wsem.at[section]).start()
                    pltpu.make_async_copy(other[turn], wv.at[section, 1 - core], wsem.at[section]).start()
            place(swapped.at[r], 3 - core, 0)
            for k in range(1, 4):
                place(near[k - 1].at[r], 2 + core, k)
                place(far[k - 1].at[r], 3 - core, k)
        return carry

    lax.fori_loop(0, 4, fetch, 0)
    head_copy = pltpu.make_async_copy(head, hv, hsem)
    head_copy.start()
    pad[...] = jnp.zeros(pad.shape, F32)
    gds[...] = jnp.zeros(gds.shape, F32)
    zero[...] = jnp.zeros(zero.shape, F32)
    total = counts[0] + counts[1] + counts[2] + counts[3]

    def push(buf, m, sem):
        q = jnp.where(m >= 7, 1, 0)
        row = pl.multiple_of((m - 7 * q) * 16, 16)
        for color in range(2):
            @pl.when(q == color)
            def _():
                for side, outs in enumerate((keeps, sends)):
                    pltpu.make_async_copy(buf.at[:, jnp.bitwise_xor(core, side)],
                                          outs[color].at[:, pl.ds(row, 16)], sem).start()

    for m in range(7, 13):
        @pl.when(m >= total)
        def _():
            push(zero, m, zsem.at[m - 7])
    image_copy.wait()
    for copy in tap_copies:
        copy.wait()

    def live_base(section):
        base = jnp.int32(0)
        for s in range(3):
            base = base + jnp.where(s < section, counts[s], 0)
        return base

    def lanes(cb):
        return pl.ds(pl.multiple_of(cb * LANE, LANE), LANE)

    def forward_cell(section, slot, n, dil):
        def block(cb, carry):
            field = xs[n, :, lanes(cb)].astype(F32)
            pad[cb, 2:18, 8:24, :] = jnp.maximum(field, 0.0).reshape(SIDE, SIDE, LANE)
            taps = dv[section, slot, :, lanes(cb)].astype(F32)
            for rb in range(4):
                mixed = jnp.zeros((4, SIDE, LANE), F32)
                for t, (a, b) in enumerate(TAPS):
                    view = pad[cb, 2 + 4 * rb + a * dil:6 + 4 * rb + a * dil, 8 + b * dil:24 + b * dil, :]
                    mixed = mixed + view * taps[t]
                us[n, 64 * rb:64 * rb + 64, lanes(cb)] = mixed.reshape(64, LANE).astype(BF16)
            return carry
        lax.fori_loop(0, 4, block, 0)
        y = jnp.dot(us[n], wv[section, slot], preferred_element_type=F32)
        xs[n + 1] = (xs[n].astype(F32) + y).astype(BF16)

    def forward_pair(p, carry):
        section = p // 2
        base = live_base(section)

        @pl.when(lax.rem(p, 2) == 0)
        def _():
            pltpu.make_async_copy(wv.at[section], wv.at[section], wsem.at[section]).wait()
        for par in range(2):
            slot = 2 * lax.rem(p, 2) + par

            @pl.when(slot < counts[section])
            def _():
                forward_cell(section, slot, base + slot, 1 + par)
        return carry

    lax.fori_loop(0, 8, forward_pair, 0)

    head_copy.wait()
    final = xs[total].astype(F32)
    pooled = jnp.sum(final, axis=0, keepdims=True) / POS
    logits = jnp.sum(hv[...] * pooled, axis=1, keepdims=True)
    classes = lax.broadcasted_iota(jnp.int32, (CLASSES, 1), 0)
    target = jnp.where(classes == labels[seg], 1.0, 0.0)
    err = (jax.nn.sigmoid(logits) - target) / 128
    back = jnp.sum(hv[...] * err, axis=0, keepdims=True) / POS
    dyb[...] = jnp.broadcast_to(back, (POS, CHAN)).astype(BF16)

    def backward_cell(section, slot, n, m, dil, par):
        dy = dyb[...]
        grad = lax.dot_general(us[n], dy, (((0,), (0,)), ((), ())), preferred_element_type=F32)
        gw[par] = grad.reshape(16, 2, 16, CHAN)
        du = lax.dot_general(dy, wv[section, slot], (((1,), (1,)), ((), ())), preferred_element_type=F32)
        du = du.astype(BF16).astype(F32)
        for cb in range(4):
            pad[cb, 2:18, 8:24, :] = du[:, cb * LANE:cb * LANE + LANE].reshape(SIDE, SIDE, LANE)

        def block(cb, carry):
            taps = dv[section, slot, :, lanes(cb)].astype(F32)
            sums = [jnp.zeros((SIDE, LANE), F32) for _ in TAPS]
            for rb in range(4):
                x = xs[n, 64 * rb:64 * rb + 64, lanes(cb)].astype(F32)
                r = jnp.maximum(x, 0.0).reshape(4, SIDE, LANE)
                acc = jnp.zeros((4, SIDE, LANE), F32)
                for t, (a, b) in enumerate(TAPS):
                    view = pad[cb, 2 + 4 * rb - a * dil:6 + 4 * rb - a * dil, 8 - b * dil:24 - b * dil, :]
                    acc = acc + view * taps[t]
                    sums[t] = sums[t] + jnp.sum(view * r, axis=0)
                old = dyb[64 * rb:64 * rb + 64, lanes(cb)].astype(F32)
                dyb[64 * rb:64 * rb + 64, lanes(cb)] = (
                    old + jnp.where(x > 0, acc.reshape(64, LANE), 0.0)).astype(BF16)
            rows = [jnp.sum(v, axis=0, keepdims=True) for v in sums]
            rows.append(jnp.zeros((7, LANE), F32))
            gds[m, :, lanes(cb)] = jnp.concatenate(rows, axis=0)
            return carry
        lax.fori_loop(0, 4, block, 0)

    def drain(par):
        pltpu.make_async_copy(gw.at[par], gw.at[par], gsem.at[par]).wait()

    def backward_pair(q, used):
        p = 7 - q
        section = p // 2
        base = live_base(section)
        used = list(used)
        for par in (1, 0):
            slot = 2 * lax.rem(p, 2) + par
            live = slot < counts[section]
            m = total - 1 - base - slot

            @pl.when(jnp.logical_and(live, used[par] > 0))
            def _():
                drain(par)

            @pl.when(live)
            def _():
                backward_cell(section, slot, base + slot, m, 1 + par, par)
                push(gw.at[par], m, gsem.at[par])
            used[par] = jnp.where(live, 1, used[par])
        return tuple(used)

    used = lax.fori_loop(0, 8, backward_pair, (jnp.int32(0), jnp.int32(0)))
    flat = jnp.concatenate([gds[m, 0:9, :] for m in range(13)] + [jnp.zeros((11, CHAN), F32)], axis=0)
    gdt[...] = jnp.transpose(flat).reshape(16, 2, 16, LANE)
    tails = []
    for side, outs in enumerate((keeps, sends)):
        mine = jnp.bitwise_xor(core, side)
        target = outs[1].at[:, pl.ds(96, 16)]
        tails.append(pltpu.make_async_copy(gdt.at[:, mine], target.at[:, :, 0:LANE], tsem.at[side, 0]))
        tails.append(pltpu.make_async_copy(zero.at[:, mine, :, 0:CHAN - LANE], target.at[:, :, LANE:CHAN],
                                           tsem.at[side, 1]))
    for copy in tails:
        copy.start()
    for par in range(2):
        @pl.when(used[par] > 0)
        def _():
            drain(par)
    for m in range(7, 13):
        @pl.when(m >= total)
        def _():
            pltpu.make_async_copy(zero, zero, zsem.at[m - 7]).wait()
    for copy in tails:
        copy.wait()


def run_step(counts, labels, images, own, weights, head):
    hbm = pl.BlockSpec(memory_space=pl.ANY)
    smem = pl.BlockSpec(memory_space=pltpu.SMEM)
    shapes = [jax.ShapeDtypeStruct((16, HALF_ROWS, CHAN), F32)] * 4
    return pl.pallas_call(
        step_kernel,
        in_specs=[smem, smem] + [hbm] * 20,
        out_specs=[hbm] * 4,
        out_shape=shapes,
        scratch_shapes=[
            pltpu.VMEM((4, 4, CHAN, CHAN), BF16),
            pltpu.VMEM((4, 4, 16, CHAN), BF16),
            pltpu.VMEM((14, POS, CHAN), BF16),
            pltpu.VMEM((13, POS, CHAN), BF16),
            pltpu.VMEM((4, 20, 32, LANE), F32),
            pltpu.VMEM((POS, CHAN), BF16),
            pltpu.VMEM((2, 16, 2, 16, CHAN), F32),
            pltpu.VMEM((16, 2, 16, CHAN), F32),
            pltpu.VMEM((13, 16, CHAN), F32),
            pltpu.VMEM((16, 2, 16, LANE), F32),
            pltpu.VMEM((CLASSES, CHAN), F32),
            pltpu.SemaphoreType.DMA((4,)),
            pltpu.SemaphoreType.DMA((4,)),
            pltpu.SemaphoreType.DMA,
            pltpu.SemaphoreType.DMA,
            pltpu.SemaphoreType.DMA((2,)),
            pltpu.SemaphoreType.DMA((6,)),
            pltpu.SemaphoreType.DMA((2, 2)),
        ],
        compiler_params=pltpu.CompilerParams(vmem_limit_bytes=56 * 1024 * 1024),
        name="step",
    )(counts, labels, images, own, *weights, head)


def finish_kernel(counts, r0, r1, r2, r3, grad_pointwise, grad_depthwise, turned):
    seg = lax.axis_index("segment")
    total = counts[0] + counts[1] + counts[2] + counts[3]
    base = jnp.int32(0)
    for s in range(3):
        base = base + jnp.where(s < seg, counts[s], 0)
    here = counts[seg]
    rows = r0[...] + r1[...] + r2[...] + r3[...]
    for j in range(4):
        grad_pointwise[j] = jnp.where(j < here, rows[48 - 16 * j:64 - 16 * j, :], 0.0)
    taps = rows[64:80, 0:LANE]
    turned[...] = jnp.transpose(taps)
    for j in range(4):
        first = jnp.maximum(total - 1 - base - j, 0) * 9
        grad_depthwise[j] = jnp.where(j < here, turned[pl.ds(first, 9), :], 0.0)


def finish(counts, parts):
    vmem = pl.BlockSpec(memory_space=pltpu.VMEM)
    return pl.pallas_call(
        finish_kernel,
        in_specs=[pl.BlockSpec(memory_space=pltpu.SMEM)] + [vmem] * 4,
        out_specs=[vmem, vmem],
        out_shape=[jax.ShapeDtypeStruct((4, 16, CHAN), F32), jax.ShapeDtypeStruct((4, 9, 16), F32)],
        scratch_shapes=[pltpu.VMEM((LANE, 16), F32)],
        name="finish",
    )(counts, *parts)


def rotate(k):
    return [(i, (i + k) % 4) for i in range(4)]


def along(axis, k):
    if axis == "x":
        return "segment", rotate(k)
    pairs = []
    for d in range(32):
        y, z, c = d // 8, d // 2 % 4, d % 2
        if axis == "y":
            y = (y + k) % 4
        elif axis == "z":
            z = (z + k) % 4
        else:
            c = c ^ 1
        pairs.append((d, y * 8 + z * 2 + c))
    return "dp", pairs


def move(value, axis, k=1):
    name, pairs = along(axis, k)
    return lax.ppermute(value, name, pairs)


def gather_weights(pointwise, depthwise, place):
    core, my_z = place["core"], place["z"]
    taps = jnp.pad(depthwise, ((0, 0), (0, 7), (0, 0)))
    direct = lax.dynamic_index_in_dim(pointwise, core, 0, keepdims=False)
    shared = lax.dynamic_slice(pointwise, (2 + core, my_z * 128, 0), (1, 128, CHAN))
    piece = jnp.concatenate([shared[0], taps.reshape(64, CHAN)], axis=0)
    pieces = [move(piece, "x", k) for k in (1, 2, 3)]
    *pieces, direct = lax.optimization_barrier([*pieces, direct])
    whole = [move(direct, "x", k) for k in (1, 2, 3)]
    stacked = jnp.stack([p[0:128] for p in pieces])
    near = [move(stacked, "z", k) for k in (1, 2, 3)]
    swapped = move(stacked, "core")
    other = [move(part, "core") for part in whole]
    far = [move(part, "core") for part in near]
    return [taps, *pieces, *whole, *other, swapped, *near, *far]


def reduce_halves(keeps, sends, orders, place):
    values = [keep + move(send, "core") for keep, send in zip(keeps, sends)]
    values = [value.reshape(4, 4, HALF_ROWS, CHAN) for value in values]
    for stage in range(2):
        pieces = []
        for value, order in zip(values, orders):
            axis = order[stage]
            dim = "yz".index(axis) if stage == 0 else 0
            pieces.append([lax.dynamic_index_in_dim(value, (place[axis] + k) % 4, dim, keepdims=False)
                           for k in range(4)])
        pieces = lax.optimization_barrier(pieces)
        moved = [[own[0]] for own in pieces]
        for k in (2, 1, 3):
            for q in range(2):
                moved[q].append(move(pieces[q][k], orders[q][stage], k))
        moved = lax.optimization_barrier(moved)
        values = [m[0] + m[1] + m[2] + m[3] for m in moved]
    return values


def local(images, labels, counts, depthwise, pointwise, head_weight):
    seg = lax.axis_index("segment")
    dp = lax.axis_index("dp")
    place = {"x": seg, "y": dp // 8, "z": dp // 2 % 4, "core": dp % 2}
    weights = gather_weights(pointwise, depthwise, place)
    outs = run_step(counts, labels, images.reshape(4, POS, CHAN), pointwise, weights, head_weight.T)
    sums = reduce_halves(outs[:2], outs[2:], ("yz", "zy"), place)
    ordered = jnp.concatenate([jnp.zeros((48, CHAN), F32), *sums], axis=0)
    total = jnp.sum(counts)
    before = jnp.cumsum(counts) - counts
    taps_rows = ordered[256:272]
    parts = []
    for k in range(4):
        dest = (seg + k) % 4
        start = (total - 1 - lax.dynamic_index_in_dim(before, dest, 0, keepdims=False)) * 16
        piece = jnp.concatenate([lax.dynamic_slice_in_dim(ordered, start, 64, 0), taps_rows], axis=0)
        parts.append(move(piece, "x", k) if k else piece)
    grad_pointwise, grad_depthwise = finish(counts, parts)
    return grad_pointwise, grad_depthwise


def solution(mesh):
    in_specs = (P("dp", None, None, None), P("dp"), P(), P("segment", None, None), P("segment", None, None), P())
    out_specs = (P("segment", "dp", None), P("segment", None, "dp"))
    return jax.shard_map(local, mesh=mesh, in_specs=in_specs, out_specs=out_specs, check_vma=False)
```

```python
import jax
import jax.numpy as jnp
from jax import lax
from jax.experimental import pallas as pl
from jax.experimental.pallas import tpu as pltpu
from jax.sharding import PartitionSpec as P

F32 = jnp.float32
BF16 = jnp.bfloat16
SIDE, POS, CHAN, LANE, CLASSES = 16, 256, 512, 128, 1000
TAPS = [(a, b) for a in (-1, 0, 1) for b in (-1, 0, 1)]
HALF_ROWS = 112


def step_kernel(counts, labels, images, own, *rest):
    own_taps, pieces, whole, other = (rest[0], rest[1:4], rest[4:7], rest[7:10])
    swapped, near, far, head = (rest[10], rest[11:14], rest[14:17], rest[17])
    keeps, sends, rest = (rest[18:20], rest[20:22], rest[22:])
    (wv, dv, xs, us, pad, dyb, gw, zero, gds, gdt, hv, wsem, dsem, isem, hsem, gsem, zsem, tsem) = rest
    seg, dp = (lax.axis_index("segment"), lax.axis_index("dp"))
    core, my_z = (lax.rem(dp, 2), lax.rem(dp // 2, 4))
    image_copy = pltpu.make_async_copy(images.at[seg], xs.at[0], isem)
    image_copy.start()
    tap_copies = [pltpu.make_async_copy(own_taps, dv.at[seg], dsem.at[0])]
    for k, piece in enumerate(pieces, 1):
        tap_copies.append(pltpu.make_async_copy(piece.at[pl.ds(128, 64)].reshape(4, 16, CHAN),
                                                dv.at[lax.rem(seg - k + 4, 4)], dsem.at[k]))
    for copy in tap_copies:
        copy.start()

    def fetch(section, carry):
        @pl.when(section == seg)
        def _():
            pltpu.make_async_copy(own, wv.at[seg], wsem.at[seg]).start()

        @pl.when(section != seg)
        def _():
            r = lax.rem(seg - section + 4, 4) - 1

            def place(part, slot, k):
                row = pl.multiple_of(lax.rem(my_z - k + 4, 4) * 128, 128)
                pltpu.make_async_copy(part, wv.at[section, slot, pl.ds(row, 128)], wsem.at[section]).start()

            for turn in range(3):
                @pl.when(r == turn)
                def _():
                    place(pieces[turn].at[pl.ds(0, 128)], 2 + core, 0)
                    pltpu.make_async_copy(whole[turn], wv.at[section, core], wsem.at[section]).start()
                    pltpu.make_async_copy(other[turn], wv.at[section, 1 - core], wsem.at[section]).start()
            place(swapped.at[r], 3 - core, 0)
            for k in range(1, 4):
                place(near[k - 1].at[r], 2 + core, k)
                place(far[k - 1].at[r], 3 - core, k)
        return carry

    lax.fori_loop(0, 4, fetch, 0)
    head_copy = pltpu.make_async_copy(head, hv, hsem)
    head_copy.start()
    pad[...] = jnp.zeros(pad.shape, F32)
    gds[...] = jnp.zeros(gds.shape, F32)
    zero[...] = jnp.zeros(zero.shape, F32)
    total = counts[0] + counts[1] + counts[2] + counts[3]

    def push(buf, m, sem):
        q = jnp.where(m >= 7, 1, 0)
        row = pl.multiple_of((m - 7 * q) * 16, 16)
        for color in range(2):
            @pl.when(q == color)
            def _():
                for side, outs in enumerate((keeps, sends)):
                    pltpu.make_async_copy(buf.at[:, jnp.bitwise_xor(core, side)],
                                          outs[color].at[:, pl.ds(row, 16)], sem).start()

    for m in range(7, 13):
        @pl.when(m >= total)
        def _():
            push(zero, m, zsem.at[m - 7])
    image_copy.wait()
    for copy in tap_copies:
        copy.wait()

    def live_base(section):
        base = jnp.int32(0)
        for s in range(3):
            base = base + jnp.where(s < section, counts[s], 0)
        return base

    def lanes(cb):
        return pl.ds(pl.multiple_of(cb * LANE, LANE), LANE)

    def forward_cell(section, slot, n, dil):
        def block(cb, carry):
            field = xs[n, :, lanes(cb)].astype(F32)
            pad[cb, 2:18, 8:24, :] = jnp.maximum(field, 0.0).reshape(SIDE, SIDE, LANE)
            taps = dv[section, slot, :, lanes(cb)].astype(F32)
            for rb in range(4):
                mixed = jnp.zeros((4, SIDE, LANE), F32)
                for t, (a, b) in enumerate(TAPS):
                    view = pad[cb, 2 + 4 * rb + a * dil:6 + 4 * rb + a * dil, 8 + b * dil:24 + b * dil, :]
                    mixed = mixed + view * taps[t]
                us[n, 64 * rb:64 * rb + 64, lanes(cb)] = mixed.reshape(64, LANE).astype(BF16)
            return carry
        lax.fori_loop(0, 4, block, 0)
        y = jnp.dot(us[n], wv[section, slot], preferred_element_type=F32)
        xs[n + 1] = (xs[n].astype(F32) + y).astype(BF16)

    def forward_pair(p, carry):
        section = p // 2
        base = live_base(section)

        @pl.when(lax.rem(p, 2) == 0)
        def _():
            pltpu.make_async_copy(wv.at[section], wv.at[section], wsem.at[section]).wait()
        for par in range(2):
            slot = 2 * lax.rem(p, 2) + par

            @pl.when(slot < counts[section])
            def _():
                forward_cell(section, slot, base + slot, 1 + par)
        return carry

    lax.fori_loop(0, 8, forward_pair, 0)

    head_copy.wait()
    final = xs[total].astype(F32)
    pooled = jnp.sum(final, axis=0, keepdims=True) / POS
    logits = jnp.sum(hv[...] * pooled, axis=1, keepdims=True)
    classes = lax.broadcasted_iota(jnp.int32, (CLASSES, 1), 0)
    target = jnp.where(classes == labels[seg], 1.0, 0.0)
    err = (jax.nn.sigmoid(logits) - target) / 128
    back = jnp.sum(hv[...] * err, axis=0, keepdims=True) / POS
    dyb[...] = jnp.broadcast_to(back, (POS, CHAN)).astype(BF16)

    def backward_cell(section, slot, n, m, dil, par):
        dy = dyb[...]
        grad = lax.dot_general(us[n], dy, (((0,), (0,)), ((), ())), preferred_element_type=F32)
        gw[par] = grad.reshape(16, 2, 16, CHAN)
        du = lax.dot_general(dy, wv[section, slot], (((1,), (1,)), ((), ())), preferred_element_type=F32)
        du = du.astype(BF16).astype(F32)
        for cb in range(4):
            pad[cb, 2:18, 8:24, :] = du[:, cb * LANE:cb * LANE + LANE].reshape(SIDE, SIDE, LANE)

        def block(cb, carry):
            taps = dv[section, slot, :, lanes(cb)].astype(F32)
            sums = [jnp.zeros((SIDE, LANE), F32) for _ in TAPS]
            for rb in range(4):
                x = xs[n, 64 * rb:64 * rb + 64, lanes(cb)].astype(F32)
                r = jnp.maximum(x, 0.0).reshape(4, SIDE, LANE)
                acc = jnp.zeros((4, SIDE, LANE), F32)
                for t, (a, b) in enumerate(TAPS):
                    view = pad[cb, 2 + 4 * rb - a * dil:6 + 4 * rb - a * dil, 8 - b * dil:24 - b * dil, :]
                    acc = acc + view * taps[t]
                    sums[t] = sums[t] + jnp.sum(view * r, axis=0)
                old = dyb[64 * rb:64 * rb + 64, lanes(cb)].astype(F32)
                dyb[64 * rb:64 * rb + 64, lanes(cb)] = (
                    old + jnp.where(x > 0, acc.reshape(64, LANE), 0.0)).astype(BF16)
            rows = [jnp.sum(v, axis=0, keepdims=True) for v in sums]
            rows.append(jnp.zeros((7, LANE), F32))
            gds[m, :, lanes(cb)] = jnp.concatenate(rows, axis=0)
            return carry
        lax.fori_loop(0, 4, block, 0)

    def drain(par):
        pltpu.make_async_copy(gw.at[par], gw.at[par], gsem.at[par]).wait()

    def backward_pair(q, used):
        p = 7 - q
        section = p // 2
        base = live_base(section)
        used = list(used)
        for par in (1, 0):
            slot = 2 * lax.rem(p, 2) + par
            live = slot < counts[section]
            m = total - 1 - base - slot

            @pl.when(jnp.logical_and(live, used[par] > 0))
            def _():
                drain(par)

            @pl.when(live)
            def _():
                backward_cell(section, slot, base + slot, m, 1 + par, par)
                push(gw.at[par], m, gsem.at[par])
            used[par] = jnp.where(live, 1, used[par])
        return tuple(used)

    used = lax.fori_loop(0, 8, backward_pair, (jnp.int32(0), jnp.int32(0)))
    flat = jnp.concatenate([gds[m, 0:9, :] for m in range(13)] + [jnp.zeros((11, CHAN), F32)], axis=0)
    gdt[...] = jnp.transpose(flat).reshape(16, 2, 16, LANE)
    tails = []
    for side, outs in enumerate((keeps, sends)):
        mine = jnp.bitwise_xor(core, side)
        target = outs[1].at[:, pl.ds(96, 16)]
        tails.append(pltpu.make_async_copy(gdt.at[:, mine], target.at[:, :, 0:LANE], tsem.at[side, 0]))
        tails.append(pltpu.make_async_copy(zero.at[:, mine, :, 0:CHAN - LANE], target.at[:, :, LANE:CHAN],
                                           tsem.at[side, 1]))
    for copy in tails:
        copy.start()
    for par in range(2):
        @pl.when(used[par] > 0)
        def _():
            drain(par)
    for m in range(7, 13):
        @pl.when(m >= total)
        def _():
            pltpu.make_async_copy(zero, zero, zsem.at[m - 7]).wait()
    for copy in tails:
        copy.wait()


def run_step(counts, labels, images, own, weights, head):
    hbm = pl.BlockSpec(memory_space=pl.ANY)
    smem = pl.BlockSpec(memory_space=pltpu.SMEM)
    shapes = [jax.ShapeDtypeStruct((16, HALF_ROWS, CHAN), F32)] * 4
    return pl.pallas_call(
        step_kernel,
        in_specs=[smem, smem] + [hbm] * 20,
        out_specs=[hbm] * 4,
        out_shape=shapes,
        scratch_shapes=[
            pltpu.VMEM((4, 4, CHAN, CHAN), BF16),
            pltpu.VMEM((4, 4, 16, CHAN), BF16),
            pltpu.VMEM((14, POS, CHAN), BF16),
            pltpu.VMEM((13, POS, CHAN), BF16),
            pltpu.VMEM((4, 20, 32, LANE), F32),
            pltpu.VMEM((POS, CHAN), BF16),
            pltpu.VMEM((2, 16, 2, 16, CHAN), F32),
            pltpu.VMEM((16, 2, 16, CHAN), F32),
            pltpu.VMEM((13, 16, CHAN), F32),
            pltpu.VMEM((16, 2, 16, LANE), F32),
            pltpu.VMEM((CLASSES, CHAN), F32),
            pltpu.SemaphoreType.DMA((4,)),
            pltpu.SemaphoreType.DMA((4,)),
            pltpu.SemaphoreType.DMA,
            pltpu.SemaphoreType.DMA,
            pltpu.SemaphoreType.DMA((2,)),
            pltpu.SemaphoreType.DMA((6,)),
            pltpu.SemaphoreType.DMA((2, 2)),
        ],
        compiler_params=pltpu.CompilerParams(vmem_limit_bytes=56 * 1024 * 1024),
        name="step",
    )(counts, labels, images, own, *weights, head)


def finish_kernel(counts, r0, r1, r2, r3, grad_pointwise, grad_depthwise, turned):
    seg = lax.axis_index("segment")
    total = counts[0] + counts[1] + counts[2] + counts[3]
    base = jnp.int32(0)
    for s in range(3):
        base = base + jnp.where(s < seg, counts[s], 0)
    here = counts[seg]
    rows = r0[...] + r1[...] + r2[...] + r3[...]
    for j in range(4):
        grad_pointwise[j] = jnp.where(j < here, rows[48 - 16 * j:64 - 16 * j, :], 0.0)
    taps = rows[64:80, 0:LANE]
    turned[...] = jnp.transpose(taps)
    for j in range(4):
        first = jnp.maximum(total - 1 - base - j, 0) * 9
        grad_depthwise[j] = jnp.where(j < here, turned[pl.ds(first, 9), :], 0.0)


def finish(counts, parts):
    vmem = pl.BlockSpec(memory_space=pltpu.VMEM)
    return pl.pallas_call(
        finish_kernel,
        in_specs=[pl.BlockSpec(memory_space=pltpu.SMEM)] + [vmem] * 4,
        out_specs=[vmem, vmem],
        out_shape=[jax.ShapeDtypeStruct((4, 16, CHAN), F32), jax.ShapeDtypeStruct((4, 9, 16), F32)],
        scratch_shapes=[pltpu.VMEM((LANE, 16), F32)],
        name="finish",
    )(counts, *parts)


def rotate(k):
    return [(i, (i + k) % 4) for i in range(4)]


def along(axis, k):
    if axis == "x":
        return "segment", rotate(k)
    pairs = []
    for d in range(32):
        y, z, c = d // 8, d // 2 % 4, d % 2
        if axis == "y":
            y = (y + k) % 4
        elif axis == "z":
            z = (z + k) % 4
        else:
            c = c ^ 1
        pairs.append((d, y * 8 + z * 2 + c))
    return "dp", pairs


def move(value, axis, k=1):
    name, pairs = along(axis, k)
    return lax.ppermute(value, name, pairs)


def gather_weights(pointwise, depthwise, place):
    core, my_z = place["core"], place["z"]
    taps = jnp.pad(depthwise, ((0, 0), (0, 7), (0, 0)))
    direct = lax.dynamic_index_in_dim(pointwise, core, 0, keepdims=False)
    shared = lax.dynamic_slice(pointwise, (2 + core, my_z * 128, 0), (1, 128, CHAN))
    piece = jnp.concatenate([shared[0], taps.reshape(64, CHAN)], axis=0)
    pieces = [move(piece, "x", k) for k in (1, 2, 3)]
    *pieces, direct = lax.optimization_barrier([*pieces, direct])
    whole = [move(direct, "x", k) for k in (1, 2, 3)]
    stacked = jnp.stack([p[0:128] for p in pieces])
    near = [move(stacked, "z", k) for k in (1, 2, 3)]
    swapped = move(stacked, "core")
    other = [move(part, "core") for part in whole]
    far = [move(part, "core") for part in near]
    return [taps, *pieces, *whole, *other, swapped, *near, *far]


def pick(value, place, axis, dim, k):
    return lax.dynamic_index_in_dim(value, (place[axis] + k) % 4, dim, keepdims=False)


def reduce_halves(keeps, sends, orders, place):
    received = [move(send, "core") for send in sends]
    received = lax.optimization_barrier(received)
    half = HALF_ROWS // 2
    pieces = []
    for keep, extra, order in zip(keeps, received, orders):
        axis, dim = order[0], "yz".index(order[0])
        keep, extra = (v.reshape(4, 4, 2, half, CHAN) for v in (keep, extra))
        whole = {k: pick(keep, place, axis, dim, k) + pick(extra, place, axis, dim, k) for k in (2, 1, 3, 0)}
        pieces.append({(k, h): whole[k][:, h] for k in whole for h in (0, 1)})
    pieces = lax.optimization_barrier(pieces)
    first = [{} for _ in pieces]
    for k, h, step in ((2, 0, 1), (2, 1, 3), (1, 1, 1), (3, 0, 3)):
        for q, order in enumerate(orders):
            first[q][k, h] = move(pieces[q][k, h], order[0], step)
    second = [{(1, 0): pieces[q][1, 0] + first[q][2, 0], (3, 1): pieces[q][3, 1] + first[q][2, 1]} for q in (0, 1)]
    second = lax.optimization_barrier(second)
    last = [{} for _ in pieces]
    for k, h in ((1, 0), (3, 1)):
        for q, order in enumerate(orders):
            last[q][k, h] = move(second[q][k, h], order[0], k)
    first, last = lax.optimization_barrier((first, last))
    values = []
    for q in (0, 1):
        low = pieces[q][0, 0] + last[q][1, 0] + first[q][3, 0]
        high = pieces[q][0, 1] + first[q][1, 1] + last[q][3, 1]
        values.append(jnp.concatenate([low, high], axis=1))
    values = lax.optimization_barrier(values)
    pieces = [[pick(value, place, order[1], 0, k) for k in range(4)] for value, order in zip(values, orders)]
    pieces = lax.optimization_barrier(pieces)
    moved = [[own[0]] for own in pieces]
    for k in (2, 1, 3):
        for q, order in enumerate(orders):
            moved[q].append(move(pieces[q][k], order[1], k))
    moved = lax.optimization_barrier(moved)
    return [m[0] + m[1] + m[2] + m[3] for m in moved]


def local(images, labels, counts, depthwise, pointwise, head_weight):
    seg = lax.axis_index("segment")
    dp = lax.axis_index("dp")
    place = {"x": seg, "y": dp // 8, "z": dp // 2 % 4, "core": dp % 2}
    weights = gather_weights(pointwise, depthwise, place)
    outs = run_step(counts, labels, images.reshape(4, POS, CHAN), pointwise, weights, head_weight.T)
    sums = reduce_halves(outs[:2], outs[2:], ("yz", "zy"), place)
    ordered = jnp.concatenate([jnp.zeros((48, CHAN), F32), *sums], axis=0)
    total = jnp.sum(counts)
    before = jnp.cumsum(counts) - counts
    taps_rows = ordered[256:272]
    parts = []
    for k in range(4):
        dest = (seg + k) % 4
        start = (total - 1 - lax.dynamic_index_in_dim(before, dest, 0, keepdims=False)) * 16
        piece = jnp.concatenate([lax.dynamic_slice_in_dim(ordered, start, 64, 0), taps_rows], axis=0)
        parts.append(move(piece, "x", k) if k else piece)
    grad_pointwise, grad_depthwise = finish(counts, parts)
    return grad_pointwise, grad_depthwise


def solution(mesh):
    in_specs = (P("dp", None, None, None), P("dp"), P(), P("segment", None, None), P("segment", None, None), P())
    out_specs = (P("segment", "dp", None), P("segment", None, "dp"))
    return jax.shard_map(local, mesh=mesh, in_specs=in_specs, out_specs=out_specs, check_vma=False)
```

```python
import jax
import jax.numpy as jnp
from jax import lax
from jax.experimental import pallas as pl
from jax.experimental.pallas import tpu as pltpu
from jax.sharding import PartitionSpec as P

F32 = jnp.float32
BF16 = jnp.bfloat16
SIDE, POS, CHAN, LANE, CLASSES = 16, 256, 512, 128, 1000
TAPS = [(a, b) for a in (-1, 0, 1) for b in (-1, 0, 1)]
HALF_ROWS = 112


def step_kernel(counts, labels, images, own, *rest):
    own_taps, pieces, whole, other = (rest[0], rest[1:4], rest[4:8], rest[8:12])
    swapped, near, far, head = (rest[12], rest[13:17], rest[17:21], rest[21])
    keeps, sends, rest = (rest[22:24], rest[24:26], rest[26:])
    (wv, dv, xs, us, pad, dyb, gw, zero, gds, gdt, hv, wsem, dsem, isem, hsem, gsem, zsem, tsem) = rest
    seg, dp = (lax.axis_index("segment"), lax.axis_index("dp"))
    core, my_z = (lax.rem(dp, 2), lax.rem(dp // 2, 4))
    image_copy = pltpu.make_async_copy(images.at[seg], xs.at[0], isem)
    image_copy.start()
    tap_copies = [pltpu.make_async_copy(own_taps, dv.at[seg], dsem.at[0])]
    for k, piece in enumerate(pieces, 1):
        tap_copies.append(pltpu.make_async_copy(piece.at[pl.ds(128, 64)].reshape(4, 16, CHAN),
                                                dv.at[lax.rem(seg - k + 4, 4)], dsem.at[k]))
    for copy in tap_copies:
        copy.start()

    def fetch(section, carry):
        @pl.when(section == seg)
        def _():
            pltpu.make_async_copy(own, wv.at[seg], wsem.at[seg]).start()

        @pl.when(section != seg)
        def _():
            r = lax.rem(seg - section + 4, 4) - 1

            def place(part, slot, first, count):
                rows = pl.ds(pl.multiple_of(first, 64), count)
                pltpu.make_async_copy(part, wv.at[section, slot, rows], wsem.at[section]).start()

            def quarter(k):
                return lax.rem(my_z - k + 4, 4) * 128

            for turn in range(3):
                @pl.when(r == turn)
                def _():
                    place(pieces[turn].at[pl.ds(0, 128)], 2 + core, quarter(0), 128)
                    for parts, slot in ((whole, core), (other, 1 - core)):
                        if turn == 1:
                            place(parts[1], slot, 0, 256)
                            place(parts[2], slot, 256, 256)
                        else:
                            place(parts[0 if turn == 0 else 3], slot, 0, 512)
            place(swapped.at[r], 3 - core, quarter(0), 128)
            for parts, slot in ((near, 2 + core), (far, 3 - core)):
                place(parts[0].at[r], slot, quarter(1), 128)
                place(parts[1].at[r], slot, quarter(2), 64)
                place(parts[2].at[r], slot, quarter(2) + 64, 64)
                place(parts[3].at[r], slot, quarter(3), 128)
        return carry

    lax.fori_loop(0, 4, fetch, 0)
    head_copy = pltpu.make_async_copy(head, hv, hsem)
    head_copy.start()
    pad[...] = jnp.zeros(pad.shape, F32)
    gds[...] = jnp.zeros(gds.shape, F32)
    zero[...] = jnp.zeros(zero.shape, F32)
    total = counts[0] + counts[1] + counts[2] + counts[3]

    def push(buf, m, sem):
        q = jnp.where(m >= 7, 1, 0)
        row = pl.multiple_of((m - 7 * q) * 16, 16)
        for color in range(2):
            @pl.when(q == color)
            def _():
                for side, outs in enumerate((keeps, sends)):
                    pltpu.make_async_copy(buf.at[:, jnp.bitwise_xor(core, side)],
                                          outs[color].at[:, pl.ds(row, 16)], sem).start()

    for m in range(7, 13):
        @pl.when(m >= total)
        def _():
            push(zero, m, zsem.at[m - 7])
    image_copy.wait()
    for copy in tap_copies:
        copy.wait()

    def live_base(section):
        base = jnp.int32(0)
        for s in range(3):
            base = base + jnp.where(s < section, counts[s], 0)
        return base

    def lanes(cb):
        return pl.ds(pl.multiple_of(cb * LANE, LANE), LANE)

    def forward_cell(section, slot, n, dil):
        def block(cb, carry):
            field = xs[n, :, lanes(cb)].astype(F32)
            pad[cb, 2:18, 8:24, :] = jnp.maximum(field, 0.0).reshape(SIDE, SIDE, LANE)
            taps = dv[section, slot, :, lanes(cb)].astype(F32)
            for rb in range(4):
                mixed = jnp.zeros((4, SIDE, LANE), F32)
                for t, (a, b) in enumerate(TAPS):
                    view = pad[cb, 2 + 4 * rb + a * dil:6 + 4 * rb + a * dil, 8 + b * dil:24 + b * dil, :]
                    mixed = mixed + view * taps[t]
                us[n, 64 * rb:64 * rb + 64, lanes(cb)] = mixed.reshape(64, LANE).astype(BF16)
            return carry
        lax.fori_loop(0, 4, block, 0)
        y = jnp.dot(us[n], wv[section, slot], preferred_element_type=F32)
        xs[n + 1] = (xs[n].astype(F32) + y).astype(BF16)

    def forward_pair(p, carry):
        section = p // 2
        base = live_base(section)

        @pl.when(lax.rem(p, 2) == 0)
        def _():
            pltpu.make_async_copy(wv.at[section], wv.at[section], wsem.at[section]).wait()
        for par in range(2):
            slot = 2 * lax.rem(p, 2) + par

            @pl.when(slot < counts[section])
            def _():
                forward_cell(section, slot, base + slot, 1 + par)
        return carry

    lax.fori_loop(0, 8, forward_pair, 0)

    head_copy.wait()
    final = xs[total].astype(F32)
    pooled = jnp.sum(final, axis=0, keepdims=True) / POS
    logits = jnp.sum(hv[...] * pooled, axis=1, keepdims=True)
    classes = lax.broadcasted_iota(jnp.int32, (CLASSES, 1), 0)
    target = jnp.where(classes == labels[seg], 1.0, 0.0)
    err = (jax.nn.sigmoid(logits) - target) / 128
    back = jnp.sum(hv[...] * err, axis=0, keepdims=True) / POS
    dyb[...] = jnp.broadcast_to(back, (POS, CHAN)).astype(BF16)

    def backward_cell(section, slot, n, m, dil, par):
        dy = dyb[...]
        grad = lax.dot_general(us[n], dy, (((0,), (0,)), ((), ())), preferred_element_type=F32)
        gw[par] = grad.reshape(16, 2, 16, CHAN)
        du = lax.dot_general(dy, wv[section, slot], (((1,), (1,)), ((), ())), preferred_element_type=F32)
        du = du.astype(BF16).astype(F32)
        for cb in range(4):
            pad[cb, 2:18, 8:24, :] = du[:, cb * LANE:cb * LANE + LANE].reshape(SIDE, SIDE, LANE)

        def block(cb, carry):
            taps = dv[section, slot, :, lanes(cb)].astype(F32)
            sums = [jnp.zeros((SIDE, LANE), F32) for _ in TAPS]
            for rb in range(4):
                x = xs[n, 64 * rb:64 * rb + 64, lanes(cb)].astype(F32)
                r = jnp.maximum(x, 0.0).reshape(4, SIDE, LANE)
                acc = jnp.zeros((4, SIDE, LANE), F32)
                for t, (a, b) in enumerate(TAPS):
                    view = pad[cb, 2 + 4 * rb - a * dil:6 + 4 * rb - a * dil, 8 - b * dil:24 - b * dil, :]
                    acc = acc + view * taps[t]
                    sums[t] = sums[t] + jnp.sum(view * r, axis=0)
                old = dyb[64 * rb:64 * rb + 64, lanes(cb)].astype(F32)
                dyb[64 * rb:64 * rb + 64, lanes(cb)] = (
                    old + jnp.where(x > 0, acc.reshape(64, LANE), 0.0)).astype(BF16)
            rows = [jnp.sum(v, axis=0, keepdims=True) for v in sums]
            rows.append(jnp.zeros((7, LANE), F32))
            gds[m, :, lanes(cb)] = jnp.concatenate(rows, axis=0)
            return carry
        lax.fori_loop(0, 4, block, 0)

    def drain(par):
        pltpu.make_async_copy(gw.at[par], gw.at[par], gsem.at[par]).wait()

    def backward_pair(q, used):
        p = 7 - q
        section = p // 2
        base = live_base(section)
        used = list(used)
        for par in (1, 0):
            slot = 2 * lax.rem(p, 2) + par
            live = slot < counts[section]
            m = total - 1 - base - slot

            @pl.when(jnp.logical_and(live, used[par] > 0))
            def _():
                drain(par)

            @pl.when(live)
            def _():
                backward_cell(section, slot, base + slot, m, 1 + par, par)
                push(gw.at[par], m, gsem.at[par])
            used[par] = jnp.where(live, 1, used[par])
        return tuple(used)

    used = lax.fori_loop(0, 8, backward_pair, (jnp.int32(0), jnp.int32(0)))
    flat = jnp.concatenate([gds[m, 0:9, :] for m in range(13)] + [jnp.zeros((11, CHAN), F32)], axis=0)
    gdt[...] = jnp.transpose(flat).reshape(16, 2, 16, LANE)
    tails = []
    for side, outs in enumerate((keeps, sends)):
        mine = jnp.bitwise_xor(core, side)
        target = outs[1].at[:, pl.ds(96, 16)]
        tails.append(pltpu.make_async_copy(gdt.at[:, mine], target.at[:, :, 0:LANE], tsem.at[side, 0]))
        tails.append(pltpu.make_async_copy(zero.at[:, mine, :, 0:CHAN - LANE], target.at[:, :, LANE:CHAN],
                                           tsem.at[side, 1]))
    for copy in tails:
        copy.start()
    for par in range(2):
        @pl.when(used[par] > 0)
        def _():
            drain(par)
    for m in range(7, 13):
        @pl.when(m >= total)
        def _():
            pltpu.make_async_copy(zero, zero, zsem.at[m - 7]).wait()
    for copy in tails:
        copy.wait()


def run_step(counts, labels, images, own, weights, head):
    hbm = pl.BlockSpec(memory_space=pl.ANY)
    smem = pl.BlockSpec(memory_space=pltpu.SMEM)
    shapes = [jax.ShapeDtypeStruct((16, HALF_ROWS, CHAN), F32)] * 4
    return pl.pallas_call(
        step_kernel,
        in_specs=[smem, smem] + [hbm] * 24,
        out_specs=[hbm] * 4,
        out_shape=shapes,
        scratch_shapes=[
            pltpu.VMEM((4, 4, CHAN, CHAN), BF16),
            pltpu.VMEM((4, 4, 16, CHAN), BF16),
            pltpu.VMEM((14, POS, CHAN), BF16),
            pltpu.VMEM((13, POS, CHAN), BF16),
            pltpu.VMEM((4, 20, 32, LANE), F32),
            pltpu.VMEM((POS, CHAN), BF16),
            pltpu.VMEM((2, 16, 2, 16, CHAN), F32),
            pltpu.VMEM((16, 2, 16, CHAN), F32),
            pltpu.VMEM((13, 16, CHAN), F32),
            pltpu.VMEM((16, 2, 16, LANE), F32),
            pltpu.VMEM((CLASSES, CHAN), F32),
            pltpu.SemaphoreType.DMA((4,)),
            pltpu.SemaphoreType.DMA((4,)),
            pltpu.SemaphoreType.DMA,
            pltpu.SemaphoreType.DMA,
            pltpu.SemaphoreType.DMA((2,)),
            pltpu.SemaphoreType.DMA((6,)),
            pltpu.SemaphoreType.DMA((2, 2)),
        ],
        compiler_params=pltpu.CompilerParams(vmem_limit_bytes=56 * 1024 * 1024),
        name="step",
    )(counts, labels, images, own, *weights, head)


def finish_kernel(counts, r0, r1, r2, r3, grad_pointwise, grad_depthwise, turned):
    seg = lax.axis_index("segment")
    total = counts[0] + counts[1] + counts[2] + counts[3]
    base = jnp.int32(0)
    for s in range(3):
        base = base + jnp.where(s < seg, counts[s], 0)
    here = counts[seg]
    rows = r0[...] + r1[...] + r2[...] + r3[...]
    for j in range(4):
        grad_pointwise[j] = jnp.where(j < here, rows[48 - 16 * j:64 - 16 * j, :], 0.0)
    taps = rows[64:80, 0:LANE]
    turned[...] = jnp.transpose(taps)
    for j in range(4):
        first = jnp.maximum(total - 1 - base - j, 0) * 9
        grad_depthwise[j] = jnp.where(j < here, turned[pl.ds(first, 9), :], 0.0)


def finish(counts, parts):
    vmem = pl.BlockSpec(memory_space=pltpu.VMEM)
    return pl.pallas_call(
        finish_kernel,
        in_specs=[pl.BlockSpec(memory_space=pltpu.SMEM)] + [vmem] * 4,
        out_specs=[vmem, vmem],
        out_shape=[jax.ShapeDtypeStruct((4, 16, CHAN), F32), jax.ShapeDtypeStruct((4, 9, 16), F32)],
        scratch_shapes=[pltpu.VMEM((LANE, 16), F32)],
        name="finish",
    )(counts, *parts)


def rotate(k):
    return [(i, (i + k) % 4) for i in range(4)]


def along(axis, k):
    if axis == "x":
        return "segment", rotate(k)
    pairs = []
    for d in range(32):
        y, z, c = d // 8, d // 2 % 4, d % 2
        if axis == "y":
            y = (y + k) % 4
        elif axis == "z":
            z = (z + k) % 4
        else:
            c = c ^ 1
        pairs.append((d, y * 8 + z * 2 + c))
    return "dp", pairs


def move(value, axis, k=1):
    name, pairs = along(axis, k)
    return lax.ppermute(value, name, pairs)


def gather_weights(pointwise, depthwise, place):
    core, my_z = place["core"], place["z"]
    taps = jnp.pad(depthwise, ((0, 0), (0, 7), (0, 0)))
    direct = lax.dynamic_index_in_dim(pointwise, core, 0, keepdims=False)
    shared = lax.dynamic_slice(pointwise, (2 + core, my_z * 128, 0), (1, 128, CHAN))
    piece = jnp.concatenate([shared[0], taps.reshape(64, CHAN)], axis=0)
    pieces = [move(piece, "x", k) for k in (1, 2, 3)]
    *pieces, direct = lax.optimization_barrier([*pieces, direct])
    whole = [move(direct, "x", 1), None, move(direct, "x", 3)]
    stacked = jnp.stack([p[0:128] for p in pieces])
    near = [move(stacked, "z", 1), None, move(stacked, "z", 3)]
    swapped = move(stacked, "core")
    whole[1:2] = [move(whole[0][0:256], "x", 1), move(whole[2][256:512], "x", 3)]
    near[1:2] = [move(near[0][:, 0:64], "z", 1), move(near[2][:, 64:128], "z", 3)]
    other = [move(part, "core") for part in whole]
    far = [move(part, "core") for part in near]
    return [taps, *pieces, *whole, *other, swapped, *near, *far]


def pick(value, place, axis, dim, k):
    return lax.dynamic_index_in_dim(value, (place[axis] + k) % 4, dim, keepdims=False)


def reduce_halves(keeps, sends, orders, place):
    received = [move(send, "core") for send in sends]
    half = HALF_ROWS // 2
    pieces = []
    for keep, extra, order in zip(keeps, received, orders):
        axis, dim = order[0], "yz".index(order[0])
        keep, extra = (v.reshape(4, 4, 2, half, CHAN) for v in (keep, extra))
        whole = {k: pick(keep, place, axis, dim, k) + pick(extra, place, axis, dim, k) for k in (2, 1, 3, 0)}
        cut = {(k, h): whole[k][:, h] for k in whole for h in (0, 1)}
        pieces.append(lax.optimization_barrier(cut))
    first = [{} for _ in pieces]
    for k, h, step in ((2, 0, 1), (2, 1, 3), (1, 1, 1), (3, 0, 3)):
        for q, order in enumerate(orders):
            first[q][k, h] = move(pieces[q][k, h], order[0], step)
    second = [{(1, 0): pieces[q][1, 0] + first[q][2, 0], (3, 1): pieces[q][3, 1] + first[q][2, 1]} for q in (0, 1)]
    second = lax.optimization_barrier(second)
    last = [{} for _ in pieces]
    for k, h in ((1, 0), (3, 1)):
        for q, order in enumerate(orders):
            last[q][k, h] = move(second[q][k, h], order[0], k)
    first, last = lax.optimization_barrier((first, last))
    values = []
    for q in (0, 1):
        low = pieces[q][0, 0] + last[q][1, 0] + first[q][3, 0]
        high = pieces[q][0, 1] + first[q][1, 1] + last[q][3, 1]
        values.append(jnp.concatenate([low, high], axis=1))
    values = lax.optimization_barrier(values)
    pieces = [[pick(value, place, order[1], 0, k) for k in range(4)] for value, order in zip(values, orders)]
    pieces = lax.optimization_barrier(pieces)
    moved = [[own[0]] for own in pieces]
    for k in (2, 1, 3):
        for q, order in enumerate(orders):
            moved[q].append(move(pieces[q][k], order[1], k))
    moved = lax.optimization_barrier(moved)
    return [m[0] + m[1] + m[2] + m[3] for m in moved]


def local(images, labels, counts, depthwise, pointwise, head_weight):
    seg = lax.axis_index("segment")
    dp = lax.axis_index("dp")
    place = {"x": seg, "y": dp // 8, "z": dp // 2 % 4, "core": dp % 2}
    weights = gather_weights(pointwise, depthwise, place)
    outs = run_step(counts, labels, images.reshape(4, POS, CHAN), pointwise, weights, head_weight.T)
    sums = reduce_halves(outs[:2], outs[2:], ("yz", "zy"), place)
    ordered = jnp.concatenate([jnp.zeros((48, CHAN), F32), *sums], axis=0)
    total = jnp.sum(counts)
    before = jnp.cumsum(counts) - counts
    taps_rows = ordered[256:272]
    parts = []
    for k in range(4):
        dest = (seg + k) % 4
        start = (total - 1 - lax.dynamic_index_in_dim(before, dest, 0, keepdims=False)) * 16
        piece = jnp.concatenate([lax.dynamic_slice_in_dim(ordered, start, 64, 0), taps_rows], axis=0)
        parts.append(move(piece, "x", k) if k else piece)
    grad_pointwise, grad_depthwise = finish(counts, parts)
    return grad_pointwise, grad_depthwise


def solution(mesh):
    in_specs = (P("dp", None, None, None), P("dp"), P(), P("segment", None, None), P("segment", None, None), P())
    out_specs = (P("segment", "dp", None), P("segment", None, "dp"))
    return jax.shard_map(local, mesh=mesh, in_specs=in_specs, out_specs=out_specs, check_vma=False)
```

```python
import jax
import jax.numpy as jnp
from jax import lax
from jax.experimental import pallas as pl
from jax.experimental.pallas import tpu as pltpu
from jax.sharding import PartitionSpec as P

F32 = jnp.float32
BF16 = jnp.bfloat16
SIDE, POS, CHAN, LANE, CLASSES = 16, 256, 512, 128, 1000
TAPS = [(a, b) for a in (-1, 0, 1) for b in (-1, 0, 1)]
HALF_ROWS = 112
HALF = 256


def step_kernel(counts, labels, images, own, *rest):
    own_taps, pieces, whole, other = (rest[0], rest[1:4], rest[4:8], rest[8:12])
    swapped, near, far, head = (rest[12], rest[13:17], rest[17:21], rest[21])
    keeps, sends, rest = (rest[22:26], rest[26:30], rest[30:])
    (wv, dv, xs, us, pad, dyb, gw, zero, gds, gdt, hv, wsem, dsem, isem, hsem, gsem, zsem, tsem) = rest
    seg, dp = (lax.axis_index("segment"), lax.axis_index("dp"))
    core, my_z = (lax.rem(dp, 2), lax.rem(dp // 2, 4))
    image_copy = pltpu.make_async_copy(images.at[seg], xs.at[0], isem)
    image_copy.start()
    tap_copies = [pltpu.make_async_copy(own_taps, dv.at[seg], dsem.at[0])]
    for k, piece in enumerate(pieces, 1):
        tap_copies.append(pltpu.make_async_copy(piece.at[pl.ds(128, 64)].reshape(4, 16, CHAN),
                                                dv.at[lax.rem(seg - k + 4, 4)], dsem.at[k]))
    for copy in tap_copies:
        copy.start()

    def fetch(section, carry):
        @pl.when(section == seg)
        def _():
            pltpu.make_async_copy(own, wv.at[seg], wsem.at[seg]).start()

        @pl.when(section != seg)
        def _():
            r = lax.rem(seg - section + 4, 4) - 1

            def place(part, slot, first, count):
                rows = pl.ds(pl.multiple_of(first, 64), count)
                pltpu.make_async_copy(part, wv.at[section, slot, rows], wsem.at[section]).start()

            def quarter(k):
                return lax.rem(my_z - k + 4, 4) * 128

            for turn in range(3):
                @pl.when(r == turn)
                def _():
                    place(pieces[turn].at[pl.ds(0, 128)], 2 + core, quarter(0), 128)
                    for parts, slot in ((whole, core), (other, 1 - core)):
                        if turn == 1:
                            place(parts[1], slot, 0, 256)
                            place(parts[2], slot, 256, 256)
                        else:
                            place(parts[0 if turn == 0 else 3], slot, 0, 512)
            place(swapped.at[r], 3 - core, quarter(0), 128)
            for parts, slot in ((near, 2 + core), (far, 3 - core)):
                place(parts[0].at[r], slot, quarter(1), 128)
                place(parts[1].at[r], slot, quarter(2), 64)
                place(parts[2].at[r], slot, quarter(2) + 64, 64)
                place(parts[3].at[r], slot, quarter(3), 128)
        return carry

    lax.fori_loop(0, 4, fetch, 0)
    head_copy = pltpu.make_async_copy(head, hv, hsem)
    head_copy.start()
    pad[...] = jnp.zeros(pad.shape, F32)
    gds[...] = jnp.zeros(gds.shape, F32)
    zero[...] = jnp.zeros(zero.shape, F32)
    total = counts[0] + counts[1] + counts[2] + counts[3]

    def push(buf, m, sem):
        q = jnp.where(m >= 7, 1, 0)
        row = pl.multiple_of((m - 7 * q) * 16, 16)
        for color in range(2):
            @pl.when(q == color)
            def _():
                for side, outs in enumerate((keeps, sends)):
                    for h in range(2):
                        pltpu.make_async_copy(
                            buf.at[:, jnp.bitwise_xor(core, side), :, HALF * h:HALF * h + HALF],
                            outs[2 * color + h].at[:, pl.ds(row, 16)], sem).start()

    for m in range(7, 13):
        @pl.when(m >= total)
        def _():
            push(zero, m, zsem.at[m - 7])
    image_copy.wait()
    for copy in tap_copies:
        copy.wait()

    def live_base(section):
        base = jnp.int32(0)
        for s in range(3):
            base = base + jnp.where(s < section, counts[s], 0)
        return base

    def lanes(cb):
        return pl.ds(pl.multiple_of(cb * LANE, LANE), LANE)

    def forward_cell(section, slot, n, dil):
        def block(cb, carry):
            field = xs[n, :, lanes(cb)].astype(F32)
            pad[cb, 2:18, 8:24, :] = jnp.maximum(field, 0.0).reshape(SIDE, SIDE, LANE)
            taps = dv[section, slot, :, lanes(cb)].astype(F32)
            for rb in range(4):
                mixed = jnp.zeros((4, SIDE, LANE), F32)
                for t, (a, b) in enumerate(TAPS):
                    view = pad[cb, 2 + 4 * rb + a * dil:6 + 4 * rb + a * dil, 8 + b * dil:24 + b * dil, :]
                    mixed = mixed + view * taps[t]
                us[n, 64 * rb:64 * rb + 64, lanes(cb)] = mixed.reshape(64, LANE).astype(BF16)
            return carry
        lax.fori_loop(0, 4, block, 0)
        y = jnp.dot(us[n], wv[section, slot], preferred_element_type=F32)
        xs[n + 1] = (xs[n].astype(F32) + y).astype(BF16)

    def forward_pair(p, carry):
        section = p // 2
        base = live_base(section)

        @pl.when(lax.rem(p, 2) == 0)
        def _():
            pltpu.make_async_copy(wv.at[section], wv.at[section], wsem.at[section]).wait()
        for par in range(2):
            slot = 2 * lax.rem(p, 2) + par

            @pl.when(slot < counts[section])
            def _():
                forward_cell(section, slot, base + slot, 1 + par)
        return carry

    lax.fori_loop(0, 8, forward_pair, 0)

    head_copy.wait()
    final = xs[total].astype(F32)
    pooled = jnp.sum(final, axis=0, keepdims=True) / POS
    logits = jnp.sum(hv[...] * pooled, axis=1, keepdims=True)
    classes = lax.broadcasted_iota(jnp.int32, (CLASSES, 1), 0)
    target = jnp.where(classes == labels[seg], 1.0, 0.0)
    err = (jax.nn.sigmoid(logits) - target) / 128
    back = jnp.sum(hv[...] * err, axis=0, keepdims=True) / POS
    dyb[...] = jnp.broadcast_to(back, (POS, CHAN)).astype(BF16)

    def backward_cell(section, slot, n, m, dil, par):
        dy = dyb[...]
        grad = lax.dot_general(us[n], dy, (((0,), (0,)), ((), ())), preferred_element_type=F32)
        gw[par] = grad.reshape(16, 2, 16, CHAN)
        du = lax.dot_general(dy, wv[section, slot], (((1,), (1,)), ((), ())), preferred_element_type=F32)
        du = du.astype(BF16).astype(F32)
        for cb in range(4):
            pad[cb, 2:18, 8:24, :] = du[:, cb * LANE:cb * LANE + LANE].reshape(SIDE, SIDE, LANE)

        def block(cb, carry):
            taps = dv[section, slot, :, lanes(cb)].astype(F32)
            sums = [jnp.zeros((SIDE, LANE), F32) for _ in TAPS]
            for rb in range(4):
                x = xs[n, 64 * rb:64 * rb + 64, lanes(cb)].astype(F32)
                r = jnp.maximum(x, 0.0).reshape(4, SIDE, LANE)
                acc = jnp.zeros((4, SIDE, LANE), F32)
                for t, (a, b) in enumerate(TAPS):
                    view = pad[cb, 2 + 4 * rb - a * dil:6 + 4 * rb - a * dil, 8 - b * dil:24 - b * dil, :]
                    acc = acc + view * taps[t]
                    sums[t] = sums[t] + jnp.sum(view * r, axis=0)
                old = dyb[64 * rb:64 * rb + 64, lanes(cb)].astype(F32)
                dyb[64 * rb:64 * rb + 64, lanes(cb)] = (
                    old + jnp.where(x > 0, acc.reshape(64, LANE), 0.0)).astype(BF16)
            rows = [jnp.sum(v, axis=0, keepdims=True) for v in sums]
            rows.append(jnp.zeros((7, LANE), F32))
            gds[m, :, lanes(cb)] = jnp.concatenate(rows, axis=0)
            return carry
        lax.fori_loop(0, 4, block, 0)

    def drain(par):
        pltpu.make_async_copy(gw.at[par], gw.at[par], gsem.at[par]).wait()

    def backward_pair(q, used):
        p = 7 - q
        section = p // 2
        base = live_base(section)
        used = list(used)
        for par in (1, 0):
            slot = 2 * lax.rem(p, 2) + par
            live = slot < counts[section]
            m = total - 1 - base - slot

            @pl.when(jnp.logical_and(live, used[par] > 0))
            def _():
                drain(par)

            @pl.when(live)
            def _():
                backward_cell(section, slot, base + slot, m, 1 + par, par)
                push(gw.at[par], m, gsem.at[par])
            used[par] = jnp.where(live, 1, used[par])
        return tuple(used)

    used = lax.fori_loop(0, 8, backward_pair, (jnp.int32(0), jnp.int32(0)))
    flat = jnp.concatenate([gds[m, 0:9, :] for m in range(13)] + [jnp.zeros((11, CHAN), F32)], axis=0)
    gdt[...] = jnp.transpose(flat).reshape(16, 2, 16, LANE)
    tails = []
    for side, outs in enumerate((keeps, sends)):
        mine = jnp.bitwise_xor(core, side)
        blocks = ((gdt.at[:, mine], outs[2].at[:, pl.ds(96, 16), 0:LANE]),
                  (zero.at[:, mine, :, 0:LANE], outs[2].at[:, pl.ds(96, 16), LANE:HALF]),
                  (zero.at[:, mine, :, 0:HALF], outs[3].at[:, pl.ds(96, 16)]))
        for i, (block, target) in enumerate(blocks):
            tails.append(pltpu.make_async_copy(block, target, tsem.at[side, i]))
    for copy in tails:
        copy.start()
    for par in range(2):
        @pl.when(used[par] > 0)
        def _():
            drain(par)
    for m in range(7, 13):
        @pl.when(m >= total)
        def _():
            pltpu.make_async_copy(zero, zero, zsem.at[m - 7]).wait()
    for copy in tails:
        copy.wait()


def run_step(counts, labels, images, own, weights, head):
    hbm = pl.BlockSpec(memory_space=pl.ANY)
    smem = pl.BlockSpec(memory_space=pltpu.SMEM)
    shapes = [jax.ShapeDtypeStruct((16, HALF_ROWS, HALF), F32)] * 8
    return pl.pallas_call(
        step_kernel,
        in_specs=[smem, smem] + [hbm] * 24,
        out_specs=[hbm] * 8,
        out_shape=shapes,
        scratch_shapes=[
            pltpu.VMEM((4, 4, CHAN, CHAN), BF16),
            pltpu.VMEM((4, 4, 16, CHAN), BF16),
            pltpu.VMEM((14, POS, CHAN), BF16),
            pltpu.VMEM((13, POS, CHAN), BF16),
            pltpu.VMEM((4, 20, 32, LANE), F32),
            pltpu.VMEM((POS, CHAN), BF16),
            pltpu.VMEM((2, 16, 2, 16, CHAN), F32),
            pltpu.VMEM((16, 2, 16, CHAN), F32),
            pltpu.VMEM((13, 16, CHAN), F32),
            pltpu.VMEM((16, 2, 16, LANE), F32),
            pltpu.VMEM((CLASSES, CHAN), F32),
            pltpu.SemaphoreType.DMA((4,)),
            pltpu.SemaphoreType.DMA((4,)),
            pltpu.SemaphoreType.DMA,
            pltpu.SemaphoreType.DMA,
            pltpu.SemaphoreType.DMA((2,)),
            pltpu.SemaphoreType.DMA((6,)),
            pltpu.SemaphoreType.DMA((2, 3)),
        ],
        compiler_params=pltpu.CompilerParams(vmem_limit_bytes=56 * 1024 * 1024),
        name="step",
    )(counts, labels, images, own, *weights, head)


def finish_kernel(counts, r0, r1, r2, r3, grad_pointwise, grad_depthwise, turned):
    seg = lax.axis_index("segment")
    total = counts[0] + counts[1] + counts[2] + counts[3]
    base = jnp.int32(0)
    for s in range(3):
        base = base + jnp.where(s < seg, counts[s], 0)
    here = counts[seg]
    rows = r0[...] + r1[...] + r2[...] + r3[...]
    for j in range(4):
        grad_pointwise[j] = jnp.where(j < here, rows[48 - 16 * j:64 - 16 * j, :], 0.0)
    taps = rows[64:80, 0:LANE]
    turned[...] = jnp.transpose(taps)
    for j in range(4):
        first = jnp.maximum(total - 1 - base - j, 0) * 9
        grad_depthwise[:, j, :] = jnp.where(j < here, turned[pl.ds(first, 9), :], 0.0)


def finish(counts, parts):
    vmem = pl.BlockSpec(memory_space=pltpu.VMEM)
    return pl.pallas_call(
        finish_kernel,
        in_specs=[pl.BlockSpec(memory_space=pltpu.SMEM)] + [vmem] * 4,
        out_specs=[vmem, vmem],
        out_shape=[jax.ShapeDtypeStruct((4, 16, CHAN), F32), jax.ShapeDtypeStruct((9, 4, 16), F32)],
        scratch_shapes=[pltpu.VMEM((LANE, 16), F32)],
        name="finish",
    )(counts, *parts)


def rotate(k):
    return [(i, (i + k) % 4) for i in range(4)]


def along(axis, k):
    if axis == "x":
        return "segment", rotate(k)
    pairs = []
    for d in range(32):
        y, z, c = d // 8, d // 2 % 4, d % 2
        if axis == "y":
            y = (y + k) % 4
        elif axis == "z":
            z = (z + k) % 4
        else:
            c = c ^ 1
        pairs.append((d, y * 8 + z * 2 + c))
    return "dp", pairs


def move(value, axis, k=1):
    name, pairs = along(axis, k)
    return lax.ppermute(value, name, pairs)


def gather_weights(pointwise, depthwise, place):
    core, my_z = place["core"], place["z"]
    taps = jnp.pad(depthwise, ((0, 0), (0, 7), (0, 0)))
    direct = lax.dynamic_index_in_dim(pointwise, core, 0, keepdims=False)
    shared = lax.dynamic_slice(pointwise, (2 + core, my_z * 128, 0), (1, 128, CHAN))
    piece = jnp.concatenate([shared[0], taps.reshape(64, CHAN)], axis=0)
    pieces = [move(piece, "x", k) for k in (1, 2, 3)]
    *pieces, direct = lax.optimization_barrier([*pieces, direct])
    whole = [move(direct, "x", 1), None, move(direct, "x", 3)]
    stacked = jnp.stack([p[0:128] for p in pieces])
    near = [move(stacked, "z", 1), None, move(stacked, "z", 3)]
    swapped = move(stacked, "core")
    whole[1:2] = [move(whole[0][0:256], "x", 1), move(whole[2][256:512], "x", 3)]
    near[1:2] = [move(near[0][:, 0:64], "z", 1), move(near[2][:, 64:128], "z", 3)]
    other = [move(part, "core") for part in whole]
    far = [move(part, "core") for part in near]
    return [taps, *pieces, *whole, *other, swapped, *near, *far]


def pick(value, place, axis, dim, k):
    return lax.dynamic_index_in_dim(value, (place[axis] + k) % 4, dim, keepdims=False)


def reduce_halves(keeps, sends, orders, place):
    received = [move(send, "core") for send in sends]
    pieces = []
    for q, order in enumerate(orders):
        axis, dim = order[0], "yz".index(order[0])
        cut = {}
        for h in (0, 1):
            keep, extra = (v[2 * q + h].reshape(4, 4, HALF_ROWS, HALF) for v in (keeps, received))
            for k in (2, 1, 3, 0):
                cut[k, h] = pick(keep, place, axis, dim, k) + pick(extra, place, axis, dim, k)
        pieces.append(lax.optimization_barrier(cut))
    first = [{} for _ in pieces]
    for k, h, step in ((2, 0, 1), (2, 1, 3), (1, 1, 1), (3, 0, 3)):
        for q, order in enumerate(orders):
            first[q][k, h] = move(pieces[q][k, h], order[0], step)
    second = [{(1, 0): pieces[q][1, 0] + first[q][2, 0], (3, 1): pieces[q][3, 1] + first[q][2, 1]} for q in (0, 1)]
    second = lax.optimization_barrier(second)
    last = [{} for _ in pieces]
    for k, h in ((1, 0), (3, 1)):
        for q, order in enumerate(orders):
            last[q][k, h] = move(second[q][k, h], order[0], k)
    first, last = lax.optimization_barrier((first, last))
    values = []
    for q in (0, 1):
        low = pieces[q][0, 0] + last[q][1, 0] + first[q][3, 0]
        high = pieces[q][0, 1] + first[q][1, 1] + last[q][3, 1]
        values.append(jnp.concatenate([low, high], axis=2))
    values = lax.optimization_barrier(values)
    pieces = [[pick(value, place, order[1], 0, k) for k in range(4)] for value, order in zip(values, orders)]
    pieces = lax.optimization_barrier(pieces)
    moved = [[own[0]] for own in pieces]
    for k in (2, 1, 3):
        for q, order in enumerate(orders):
            moved[q].append(move(pieces[q][k], order[1], k))
    moved = lax.optimization_barrier(moved)
    return [m[0] + m[1] + m[2] + m[3] for m in moved]


def local(images, labels, counts, depthwise, pointwise, head_weight):
    seg = lax.axis_index("segment")
    dp = lax.axis_index("dp")
    place = {"x": seg, "y": dp // 8, "z": dp // 2 % 4, "core": dp % 2}
    weights = gather_weights(pointwise, depthwise, place)
    outs = run_step(counts, labels, images.reshape(4, POS, CHAN), pointwise, weights, head_weight.T)
    sums = reduce_halves(outs[:4], outs[4:], ("yz", "zy"), place)
    ordered = jnp.concatenate([jnp.zeros((48, CHAN), F32), *sums], axis=0)
    total = jnp.sum(counts)
    before = jnp.cumsum(counts) - counts
    taps_rows = ordered[256:272]
    parts = []
    for k in range(4):
        dest = (seg + k) % 4
        start = (total - 1 - lax.dynamic_index_in_dim(before, dest, 0, keepdims=False)) * 16
        piece = jnp.concatenate([lax.dynamic_slice_in_dim(ordered, start, 64, 0), taps_rows], axis=0)
        parts.append(move(piece, "x", k) if k else piece)
    grad_pointwise, grad_depthwise = finish(counts, parts)
    return grad_pointwise, jnp.transpose(grad_depthwise, (1, 0, 2))


def solution(mesh):
    in_specs = (P("dp", None, None, None), P("dp"), P(), P("segment", None, None), P("segment", None, None), P())
    out_specs = (P("segment", "dp", None), P("segment", None, "dp"))
    return jax.shard_map(local, mesh=mesh, in_specs=in_specs, out_specs=out_specs, check_vma=False)
```

```python
import jax
import jax.numpy as jnp
from jax import lax
from jax.experimental import pallas as pl
from jax.experimental.pallas import tpu as pltpu
from jax.sharding import PartitionSpec as P

F32 = jnp.float32
BF16 = jnp.bfloat16
SIDE, POS, CHAN, LANE, CLASSES = 16, 256, 512, 128, 1000
TAPS = [(a, b) for a in (-1, 0, 1) for b in (-1, 0, 1)]
COLOR_ROWS = (128, 96)
HALF = 256


def step_kernel(counts, labels, images, own, *rest):
    own_taps, pieces, whole, other = (rest[0], rest[1:4], rest[4:8], rest[8:12])
    swapped, near, far, head = (rest[12], rest[13:17], rest[17:21], rest[21])
    keeps, sends, rest = (rest[22:26], rest[26:30], rest[30:])
    (wv, dv, xs, us, pad, dyb, gw, zero, gds, gdt, hv, wsem, dsem, isem, hsem, gsem, zsem, tsem) = rest
    seg, dp = (lax.axis_index("segment"), lax.axis_index("dp"))
    core, my_z = (lax.rem(dp, 2), lax.rem(dp // 2, 4))
    image_copy = pltpu.make_async_copy(images.at[seg], xs.at[0], isem)
    image_copy.start()
    tap_copies = [pltpu.make_async_copy(own_taps, dv.at[seg], dsem.at[0])]
    for k, piece in enumerate(pieces, 1):
        tap_copies.append(pltpu.make_async_copy(piece.at[pl.ds(128, 64)].reshape(4, 16, CHAN),
                                                dv.at[lax.rem(seg - k + 4, 4)], dsem.at[k]))
    for copy in tap_copies:
        copy.start()

    def fetch(section, carry):
        @pl.when(section == seg)
        def _():
            pltpu.make_async_copy(own, wv.at[seg], wsem.at[seg]).start()

        @pl.when(section != seg)
        def _():
            r = lax.rem(seg - section + 4, 4) - 1

            def place(part, slot, first, count):
                rows = pl.ds(pl.multiple_of(first, 64), count)
                pltpu.make_async_copy(part, wv.at[section, slot, rows], wsem.at[section]).start()

            def quarter(k):
                return lax.rem(my_z - k + 4, 4) * 128

            for turn in range(3):
                @pl.when(r == turn)
                def _():
                    place(pieces[turn].at[pl.ds(0, 128)], 2 + core, quarter(0), 128)
                    for parts, slot in ((whole, core), (other, 1 - core)):
                        if turn == 1:
                            place(parts[1], slot, 0, 256)
                            place(parts[2], slot, 256, 256)
                        else:
                            place(parts[0 if turn == 0 else 3], slot, 0, 512)
            place(swapped.at[r], 3 - core, quarter(0), 128)
            for parts, slot in ((near, 2 + core), (far, 3 - core)):
                place(parts[0].at[r], slot, quarter(1), 128)
                place(parts[1].at[r], slot, quarter(2), 64)
                place(parts[2].at[r], slot, quarter(2) + 64, 64)
                place(parts[3].at[r], slot, quarter(3), 128)
        return carry

    lax.fori_loop(0, 4, fetch, 0)
    head_copy = pltpu.make_async_copy(head, hv, hsem)
    head_copy.start()
    pad[...] = jnp.zeros(pad.shape, F32)
    gds[...] = jnp.zeros(gds.shape, F32)
    zero[...] = jnp.zeros(zero.shape, F32)
    total = counts[0] + counts[1] + counts[2] + counts[3]

    def push(buf, m, sem):
        q = jnp.where(m >= 8, 1, 0)
        row = pl.multiple_of((m - 8 * q) * 16, 16)
        for color in range(2):
            @pl.when(q == color)
            def _():
                for side, outs in enumerate((keeps, sends)):
                    for h in range(2):
                        pltpu.make_async_copy(
                            buf.at[:, jnp.bitwise_xor(core, side), :, HALF * h:HALF * h + HALF],
                            outs[2 * color + h].at[:, pl.ds(row, 16)], sem).start()

    for m in range(7, 13):
        @pl.when(m >= total)
        def _():
            push(zero, m, zsem.at[m - 7])
    image_copy.wait()
    for copy in tap_copies:
        copy.wait()

    def live_base(section):
        base = jnp.int32(0)
        for s in range(3):
            base = base + jnp.where(s < section, counts[s], 0)
        return base

    def lanes(cb):
        return pl.ds(pl.multiple_of(cb * LANE, LANE), LANE)

    def forward_cell(section, slot, n, dil):
        def block(cb, carry):
            field = xs[n, :, lanes(cb)].astype(F32)
            pad[cb, 2:18, 8:24, :] = jnp.maximum(field, 0.0).reshape(SIDE, SIDE, LANE)
            taps = dv[section, slot, :, lanes(cb)].astype(F32)
            for rb in range(4):
                mixed = jnp.zeros((4, SIDE, LANE), F32)
                for t, (a, b) in enumerate(TAPS):
                    view = pad[cb, 2 + 4 * rb + a * dil:6 + 4 * rb + a * dil, 8 + b * dil:24 + b * dil, :]
                    mixed = mixed + view * taps[t]
                us[n, 64 * rb:64 * rb + 64, lanes(cb)] = mixed.reshape(64, LANE).astype(BF16)
            return carry
        lax.fori_loop(0, 4, block, 0)
        y = jnp.dot(us[n], wv[section, slot], preferred_element_type=F32)
        xs[n + 1] = (xs[n].astype(F32) + y).astype(BF16)

    def forward_pair(p, carry):
        section = p // 2
        base = live_base(section)

        @pl.when(lax.rem(p, 2) == 0)
        def _():
            pltpu.make_async_copy(wv.at[section], wv.at[section], wsem.at[section]).wait()
        for par in range(2):
            slot = 2 * lax.rem(p, 2) + par

            @pl.when(slot < counts[section])
            def _():
                forward_cell(section, slot, base + slot, 1 + par)
        return carry

    lax.fori_loop(0, 8, forward_pair, 0)

    head_copy.wait()
    final = xs[total].astype(F32)
    pooled = jnp.sum(final, axis=0, keepdims=True) / POS
    logits = jnp.sum(hv[...] * pooled, axis=1, keepdims=True)
    classes = lax.broadcasted_iota(jnp.int32, (CLASSES, 1), 0)
    target = jnp.where(classes == labels[seg], 1.0, 0.0)
    err = (jax.nn.sigmoid(logits) - target) / 128
    back = jnp.sum(hv[...] * err, axis=0, keepdims=True) / POS
    dyb[...] = jnp.broadcast_to(back, (POS, CHAN)).astype(BF16)

    def backward_cell(section, slot, n, m, dil, par):
        dy = dyb[...]
        grad = lax.dot_general(us[n], dy, (((0,), (0,)), ((), ())), preferred_element_type=F32)
        gw[par] = grad.reshape(16, 2, 16, CHAN)
        du = lax.dot_general(dy, wv[section, slot], (((1,), (1,)), ((), ())), preferred_element_type=F32)
        du = du.astype(BF16).astype(F32)
        for cb in range(4):
            pad[cb, 2:18, 8:24, :] = du[:, cb * LANE:cb * LANE + LANE].reshape(SIDE, SIDE, LANE)

        def block(cb, carry):
            taps = dv[section, slot, :, lanes(cb)].astype(F32)
            sums = [jnp.zeros((SIDE, LANE), F32) for _ in TAPS]
            for rb in range(4):
                x = xs[n, 64 * rb:64 * rb + 64, lanes(cb)].astype(F32)
                r = jnp.maximum(x, 0.0).reshape(4, SIDE, LANE)
                acc = jnp.zeros((4, SIDE, LANE), F32)
                for t, (a, b) in enumerate(TAPS):
                    view = pad[cb, 2 + 4 * rb - a * dil:6 + 4 * rb - a * dil, 8 - b * dil:24 - b * dil, :]
                    acc = acc + view * taps[t]
                    sums[t] = sums[t] + jnp.sum(view * r, axis=0)
                old = dyb[64 * rb:64 * rb + 64, lanes(cb)].astype(F32)
                dyb[64 * rb:64 * rb + 64, lanes(cb)] = (
                    old + jnp.where(x > 0, acc.reshape(64, LANE), 0.0)).astype(BF16)
            rows = [jnp.sum(v, axis=0, keepdims=True) for v in sums]
            rows.append(jnp.zeros((7, LANE), F32))
            gds[m, :, lanes(cb)] = jnp.concatenate(rows, axis=0)
            return carry
        lax.fori_loop(0, 4, block, 0)

    def drain(par):
        pltpu.make_async_copy(gw.at[par], gw.at[par], gsem.at[par]).wait()

    def backward_pair(q, used):
        p = 7 - q
        section = p // 2
        base = live_base(section)
        used = list(used)
        for par in (1, 0):
            slot = 2 * lax.rem(p, 2) + par
            live = slot < counts[section]
            m = total - 1 - base - slot

            @pl.when(jnp.logical_and(live, used[par] > 0))
            def _():
                drain(par)

            @pl.when(live)
            def _():
                backward_cell(section, slot, base + slot, m, 1 + par, par)
                push(gw.at[par], m, gsem.at[par])
            used[par] = jnp.where(live, 1, used[par])
        return tuple(used)

    used = lax.fori_loop(0, 8, backward_pair, (jnp.int32(0), jnp.int32(0)))
    flat = jnp.concatenate([gds[m, 0:9, :] for m in range(13)] + [jnp.zeros((11, CHAN), F32)], axis=0)
    gdt[...] = jnp.transpose(flat).reshape(16, 2, 16, LANE)
    tails = []
    for side, outs in enumerate((keeps, sends)):
        mine = jnp.bitwise_xor(core, side)
        blocks = ((gdt.at[:, mine], outs[2].at[:, pl.ds(80, 16), 0:LANE]),
                  (zero.at[:, mine, :, 0:LANE], outs[2].at[:, pl.ds(80, 16), LANE:HALF]),
                  (zero.at[:, mine, :, 0:HALF], outs[3].at[:, pl.ds(80, 16)]))
        for i, (block, target) in enumerate(blocks):
            tails.append(pltpu.make_async_copy(block, target, tsem.at[side, i]))
    for copy in tails:
        copy.start()
    for par in range(2):
        @pl.when(used[par] > 0)
        def _():
            drain(par)
    for m in range(7, 13):
        @pl.when(m >= total)
        def _():
            pltpu.make_async_copy(zero, zero, zsem.at[m - 7]).wait()
    for copy in tails:
        copy.wait()


def run_step(counts, labels, images, own, weights, head):
    hbm = pl.BlockSpec(memory_space=pl.ANY)
    smem = pl.BlockSpec(memory_space=pltpu.SMEM)
    shapes = [jax.ShapeDtypeStruct((16, rows, HALF), F32) for rows in (128, 128, 96, 96)] * 2
    return pl.pallas_call(
        step_kernel,
        in_specs=[smem, smem] + [hbm] * 24,
        out_specs=[hbm] * 8,
        out_shape=shapes,
        scratch_shapes=[
            pltpu.VMEM((4, 4, CHAN, CHAN), BF16),
            pltpu.VMEM((4, 4, 16, CHAN), BF16),
            pltpu.VMEM((14, POS, CHAN), BF16),
            pltpu.VMEM((13, POS, CHAN), BF16),
            pltpu.VMEM((4, 20, 32, LANE), F32),
            pltpu.VMEM((POS, CHAN), BF16),
            pltpu.VMEM((2, 16, 2, 16, CHAN), F32),
            pltpu.VMEM((16, 2, 16, CHAN), F32),
            pltpu.VMEM((13, 16, CHAN), F32),
            pltpu.VMEM((16, 2, 16, LANE), F32),
            pltpu.VMEM((CLASSES, CHAN), F32),
            pltpu.SemaphoreType.DMA((4,)),
            pltpu.SemaphoreType.DMA((4,)),
            pltpu.SemaphoreType.DMA,
            pltpu.SemaphoreType.DMA,
            pltpu.SemaphoreType.DMA((2,)),
            pltpu.SemaphoreType.DMA((6,)),
            pltpu.SemaphoreType.DMA((2, 3)),
        ],
        compiler_params=pltpu.CompilerParams(vmem_limit_bytes=56 * 1024 * 1024),
        name="step",
    )(counts, labels, images, own, *weights, head)


def finish_kernel(counts, r0, r1, r2, r3, grad_pointwise, grad_depthwise, turned):
    seg = lax.axis_index("segment")
    total = counts[0] + counts[1] + counts[2] + counts[3]
    base = jnp.int32(0)
    for s in range(3):
        base = base + jnp.where(s < seg, counts[s], 0)
    here = counts[seg]
    rows = r0[...] + r1[...] + r2[...] + r3[...]
    for j in range(4):
        grad_pointwise[j] = jnp.where(j < here, rows[48 - 16 * j:64 - 16 * j, :], 0.0)
    taps = rows[64:80, 0:LANE]
    turned[...] = jnp.transpose(taps)
    for j in range(4):
        first = jnp.maximum(total - 1 - base - j, 0) * 9
        grad_depthwise[:, j, :] = jnp.where(j < here, turned[pl.ds(first, 9), :], 0.0)


def finish(counts, parts):
    vmem = pl.BlockSpec(memory_space=pltpu.VMEM)
    return pl.pallas_call(
        finish_kernel,
        in_specs=[pl.BlockSpec(memory_space=pltpu.SMEM)] + [vmem] * 4,
        out_specs=[vmem, vmem],
        out_shape=[jax.ShapeDtypeStruct((4, 16, CHAN), F32), jax.ShapeDtypeStruct((9, 4, 16), F32)],
        scratch_shapes=[pltpu.VMEM((LANE, 16), F32)],
        name="finish",
    )(counts, *parts)


def rotate(k):
    return [(i, (i + k) % 4) for i in range(4)]


def along(axis, k):
    if axis == "x":
        return "segment", rotate(k)
    pairs = []
    for d in range(32):
        y, z, c = d // 8, d // 2 % 4, d % 2
        if axis == "y":
            y = (y + k) % 4
        elif axis == "z":
            z = (z + k) % 4
        else:
            c = c ^ 1
        pairs.append((d, y * 8 + z * 2 + c))
    return "dp", pairs


def move(value, axis, k=1):
    name, pairs = along(axis, k)
    return lax.ppermute(value, name, pairs)


def gather_weights(pointwise, depthwise, place):
    core, my_z = place["core"], place["z"]
    taps = jnp.pad(depthwise, ((0, 0), (0, 7), (0, 0)))
    direct = lax.dynamic_index_in_dim(pointwise, core, 0, keepdims=False)
    shared = lax.dynamic_slice(pointwise, (2 + core, my_z * 128, 0), (1, 128, CHAN))
    piece = jnp.concatenate([shared[0], taps.reshape(64, CHAN)], axis=0)
    pieces = [move(piece, "x", k) for k in (1, 2, 3)]
    *pieces, direct = lax.optimization_barrier([*pieces, direct])
    whole = [move(direct, "x", 1), None, move(direct, "x", 3)]
    stacked = jnp.stack([p[0:128] for p in pieces])
    near = [move(stacked, "z", 1), None, move(stacked, "z", 3)]
    swapped = move(stacked, "core")
    whole[1:2] = [move(whole[0][0:256], "x", 1), move(whole[2][256:512], "x", 3)]
    near[1:2] = [move(near[0][:, 0:64], "z", 1), move(near[2][:, 64:128], "z", 3)]
    other = [move(part, "core") for part in whole]
    far = [move(part, "core") for part in near]
    return [taps, *pieces, *whole, *other, swapped, *near, *far]


def pick(value, place, axis, dim, k):
    return lax.dynamic_index_in_dim(value, (place[axis] + k) % 4, dim, keepdims=False)


def reduce_halves(keeps, sends, orders, place):
    received = [move(send, "core") for send in sends]
    pieces = []
    for q, order in enumerate(orders):
        axis, dim = order[0], "yz".index(order[0])
        cut = {}
        for h in (0, 1):
            keep, extra = (v[2 * q + h].reshape(4, 4, COLOR_ROWS[q], HALF) for v in (keeps, received))
            for k in (2, 1, 3, 0):
                cut[k, h] = pick(keep, place, axis, dim, k) + pick(extra, place, axis, dim, k)
        pieces.append(lax.optimization_barrier(cut))
    first = [{} for _ in pieces]
    for k, h, step in ((2, 0, 1), (2, 1, 3), (1, 1, 1), (3, 0, 3)):
        for q, order in enumerate(orders):
            first[q][k, h] = move(pieces[q][k, h], order[0], step)
    second = [{(1, 0): pieces[q][1, 0] + first[q][2, 0], (3, 1): pieces[q][3, 1] + first[q][2, 1]} for q in (0, 1)]
    second = [lax.optimization_barrier(part) for part in second]
    last = [{} for _ in pieces]
    for k, h in ((1, 0), (3, 1)):
        for q, order in enumerate(orders):
            last[q][k, h] = move(second[q][k, h], order[0], k)
    first, last = lax.optimization_barrier((first, last))
    values = []
    for q in (0, 1):
        low = pieces[q][0, 0] + last[q][1, 0] + first[q][3, 0]
        high = pieces[q][0, 1] + first[q][1, 1] + last[q][3, 1]
        values.append(jnp.concatenate([low, high], axis=2))
    values = lax.optimization_barrier(values)
    pieces = [[pick(value, place, order[1], 0, k) for k in range(4)] for value, order in zip(values, orders)]
    pieces = lax.optimization_barrier(pieces)
    moved = [[own[0]] for own in pieces]
    for k in (2, 1, 3):
        for q, order in enumerate(orders):
            moved[q].append(move(pieces[q][k], order[1], k))
    moved = lax.optimization_barrier(moved)
    return [m[0] + m[1] + m[2] + m[3] for m in moved]


def local(images, labels, counts, depthwise, pointwise, head_weight):
    seg = lax.axis_index("segment")
    dp = lax.axis_index("dp")
    place = {"x": seg, "y": dp // 8, "z": dp // 2 % 4, "core": dp % 2}
    weights = gather_weights(pointwise, depthwise, place)
    outs = run_step(counts, labels, images.reshape(4, POS, CHAN), pointwise, weights, head_weight.T)
    sums = reduce_halves(outs[:4], outs[4:], ("yz", "zy"), place)
    ordered = jnp.concatenate([jnp.zeros((48, CHAN), F32), *sums], axis=0)
    total = jnp.sum(counts)
    before = jnp.cumsum(counts) - counts
    taps_rows = ordered[256:272]
    parts = []
    for k in range(4):
        dest = (seg + k) % 4
        start = (total - 1 - lax.dynamic_index_in_dim(before, dest, 0, keepdims=False)) * 16
        piece = jnp.concatenate([lax.dynamic_slice_in_dim(ordered, start, 64, 0), taps_rows], axis=0)
        parts.append(move(piece, "x", k) if k else piece)
    grad_pointwise, grad_depthwise = finish(counts, parts)
    return grad_pointwise, jnp.transpose(grad_depthwise, (1, 0, 2))


def solution(mesh):
    in_specs = (P("dp", None, None, None), P("dp"), P(), P("segment", None, None), P("segment", None, None), P())
    out_specs = (P("segment", "dp", None), P("segment", None, "dp"))
    return jax.shard_map(local, mesh=mesh, in_specs=in_specs, out_specs=out_specs, check_vma=False)
```

```python
import jax
import jax.numpy as jnp
from jax import lax
from jax.experimental import pallas as pl
from jax.experimental.pallas import tpu as pltpu
from jax.sharding import PartitionSpec as P

F32 = jnp.float32
BF16 = jnp.bfloat16
SIDE, POS, CHAN, LANE, CLASSES = 16, 256, 512, 128, 1000
TAPS = [(a, b) for a in (-1, 0, 1) for b in (-1, 0, 1)]
COLOR_ROWS = (128, 96)
HALF = 256


def step_kernel(counts, labels, images, own, *rest):
    own_taps, pieces, whole, other = (rest[0], rest[1:4], rest[4:8], rest[8:12])
    swapped, near, far, head = (rest[12], rest[13:17], rest[17:21], rest[21])
    keeps, sends, rest = (rest[22:26], rest[26:30], rest[30:])
    (wv, dv, xs, us, pad, dyb, gw, zero, gds, gdt, hv, wsem, dsem, isem, hsem, gsem, zsem, tsem) = rest
    seg, dp = (lax.axis_index("segment"), lax.axis_index("dp"))
    core, my_z = (lax.rem(dp, 2), lax.rem(dp // 2, 4))
    image_copy = pltpu.make_async_copy(images.at[seg], xs.at[0], isem)
    image_copy.start()
    tap_copies = [pltpu.make_async_copy(own_taps, dv.at[seg], dsem.at[0])]
    for k, piece in enumerate(pieces, 1):
        tap_copies.append(pltpu.make_async_copy(piece.at[pl.ds(128, 64)].reshape(4, 16, CHAN),
                                                dv.at[lax.rem(seg - k + 4, 4)], dsem.at[k]))
    for copy in tap_copies:
        copy.start()

    def fetch(section, carry):
        @pl.when(section == seg)
        def _():
            pltpu.make_async_copy(own, wv.at[seg], wsem.at[seg]).start()

        @pl.when(section != seg)
        def _():
            r = lax.rem(seg - section + 4, 4) - 1

            def place(part, slot, first, count):
                rows = pl.ds(pl.multiple_of(first, 64), count)
                pltpu.make_async_copy(part, wv.at[section, slot, rows], wsem.at[section]).start()

            def quarter(k):
                return lax.rem(my_z - k + 4, 4) * 128

            for turn in range(3):
                @pl.when(r == turn)
                def _():
                    place(pieces[turn].at[pl.ds(0, 128)], 2 + core, quarter(0), 128)
                    for parts, slot in ((whole, core), (other, 1 - core)):
                        if turn == 1:
                            place(parts[1], slot, 0, 256)
                            place(parts[2], slot, 256, 256)
                        else:
                            place(parts[0 if turn == 0 else 3], slot, 0, 512)
            place(swapped.at[r], 3 - core, quarter(0), 128)
            for parts, slot in ((near, 2 + core), (far, 3 - core)):
                place(parts[0].at[r], slot, quarter(1), 128)
                place(parts[1].at[r], slot, quarter(2), 64)
                place(parts[2].at[r], slot, quarter(2) + 64, 64)
                place(parts[3].at[r], slot, quarter(3), 128)
        return carry

    lax.fori_loop(0, 4, fetch, 0)
    head_copy = pltpu.make_async_copy(head, hv, hsem)
    head_copy.start()
    pad[...] = jnp.zeros(pad.shape, F32)
    gds[...] = jnp.zeros(gds.shape, F32)
    zero[...] = jnp.zeros(zero.shape, F32)
    total = counts[0] + counts[1] + counts[2] + counts[3]

    def push(buf, m, sem):
        q = jnp.where(m >= 8, 1, 0)
        row = pl.multiple_of((m - 8 * q) * 16, 16)
        for color in range(2):
            @pl.when(q == color)
            def _():
                for side, outs in enumerate((keeps, sends)):
                    for h in range(2):
                        pltpu.make_async_copy(
                            buf.at[:, jnp.bitwise_xor(core, side), :, HALF * h:HALF * h + HALF],
                            outs[2 * color + h].at[:, pl.ds(row, 16)], sem).start()

    for m in range(7, 13):
        @pl.when(m >= total)
        def _():
            push(zero, m, zsem.at[m - 7])
    image_copy.wait()
    for copy in tap_copies:
        copy.wait()

    def live_base(section):
        base = jnp.int32(0)
        for s in range(3):
            base = base + jnp.where(s < section, counts[s], 0)
        return base

    def lanes(cb):
        return pl.ds(pl.multiple_of(cb * LANE, LANE), LANE)

    def forward_cell(section, slot, n, dil):
        def block(cb, carry):
            field = xs[n, :, lanes(cb)].astype(F32)
            pad[cb, 2:18, 8:24, :] = jnp.maximum(field, 0.0).reshape(SIDE, SIDE, LANE)
            taps = dv[section, slot, :, lanes(cb)].astype(F32)
            for rb in range(4):
                mixed = jnp.zeros((4, SIDE, LANE), F32)
                for t, (a, b) in enumerate(TAPS):
                    view = pad[cb, 2 + 4 * rb + a * dil:6 + 4 * rb + a * dil, 8 + b * dil:24 + b * dil, :]
                    mixed = mixed + view * taps[t]
                us[n, 64 * rb:64 * rb + 64, lanes(cb)] = mixed.reshape(64, LANE).astype(BF16)
            return carry
        lax.fori_loop(0, 4, block, 0)
        y = jnp.dot(us[n], wv[section, slot], preferred_element_type=F32)
        xs[n + 1] = (xs[n].astype(F32) + y).astype(BF16)

    def forward_pair(p, carry):
        section = p // 2
        base = live_base(section)

        @pl.when(lax.rem(p, 2) == 0)
        def _():
            pltpu.make_async_copy(wv.at[section], wv.at[section], wsem.at[section]).wait()
        for par in range(2):
            slot = 2 * lax.rem(p, 2) + par

            @pl.when(slot < counts[section])
            def _():
                forward_cell(section, slot, base + slot, 1 + par)
        return carry

    lax.fori_loop(0, 8, forward_pair, 0)

    head_copy.wait()
    final = xs[total].astype(F32)
    pooled = jnp.sum(final, axis=0, keepdims=True) / POS
    logits = jnp.sum(hv[...] * pooled, axis=1, keepdims=True)
    classes = lax.broadcasted_iota(jnp.int32, (CLASSES, 1), 0)
    target = jnp.where(classes == labels[seg], 1.0, 0.0)
    err = (jax.nn.sigmoid(logits) - target) / 128
    back = jnp.sum(hv[...] * err, axis=0, keepdims=True) / POS
    dyb[...] = jnp.broadcast_to(back, (POS, CHAN)).astype(BF16)

    def backward_cell(section, slot, n, m, dil, par):
        dy = dyb[...]
        grad = lax.dot_general(us[n], dy, (((0,), (0,)), ((), ())), preferred_element_type=F32)
        gw[par] = grad.reshape(16, 2, 16, CHAN)
        du = lax.dot_general(dy, wv[section, slot], (((1,), (1,)), ((), ())), preferred_element_type=F32)
        du = du.astype(BF16).astype(F32)
        for cb in range(4):
            pad[cb, 2:18, 8:24, :] = du[:, cb * LANE:cb * LANE + LANE].reshape(SIDE, SIDE, LANE)

        def block(cb, carry):
            taps = dv[section, slot, :, lanes(cb)].astype(F32)
            sums = [jnp.zeros((SIDE, LANE), F32) for _ in TAPS]
            for rb in range(4):
                x = xs[n, 64 * rb:64 * rb + 64, lanes(cb)].astype(F32)
                r = jnp.maximum(x, 0.0).reshape(4, SIDE, LANE)
                acc = jnp.zeros((4, SIDE, LANE), F32)
                for t, (a, b) in enumerate(TAPS):
                    view = pad[cb, 2 + 4 * rb - a * dil:6 + 4 * rb - a * dil, 8 - b * dil:24 - b * dil, :]
                    acc = acc + view * taps[t]
                    sums[t] = sums[t] + jnp.sum(view * r, axis=0)
                old = dyb[64 * rb:64 * rb + 64, lanes(cb)].astype(F32)
                dyb[64 * rb:64 * rb + 64, lanes(cb)] = (
                    old + jnp.where(x > 0, acc.reshape(64, LANE), 0.0)).astype(BF16)
            rows = [jnp.sum(v, axis=0, keepdims=True) for v in sums]
            rows.append(jnp.zeros((7, LANE), F32))
            gds[m, :, lanes(cb)] = jnp.concatenate(rows, axis=0)
            return carry
        lax.fori_loop(0, 4, block, 0)

    def drain(par):
        pltpu.make_async_copy(gw.at[par], gw.at[par], gsem.at[par]).wait()

    def backward_pair(q, used):
        p = 7 - q
        section = p // 2
        base = live_base(section)
        used = list(used)
        for par in (1, 0):
            slot = 2 * lax.rem(p, 2) + par
            live = slot < counts[section]
            m = total - 1 - base - slot

            @pl.when(jnp.logical_and(live, used[par] > 0))
            def _():
                drain(par)

            @pl.when(live)
            def _():
                backward_cell(section, slot, base + slot, m, 1 + par, par)
                push(gw.at[par], m, gsem.at[par])
            used[par] = jnp.where(live, 1, used[par])
        return tuple(used)

    used = lax.fori_loop(0, 8, backward_pair, (jnp.int32(0), jnp.int32(0)))
    flat = jnp.concatenate([gds[m, 0:9, :] for m in range(13)] + [jnp.zeros((11, CHAN), F32)], axis=0)
    gdt[...] = jnp.transpose(flat).reshape(16, 2, 16, LANE)
    tails = []
    for side, outs in enumerate((keeps, sends)):
        mine = jnp.bitwise_xor(core, side)
        blocks = ((gdt.at[:, mine], outs[2].at[:, pl.ds(80, 16), 0:LANE]),
                  (zero.at[:, mine, :, 0:LANE], outs[2].at[:, pl.ds(80, 16), LANE:HALF]),
                  (zero.at[:, mine, :, 0:HALF], outs[3].at[:, pl.ds(80, 16)]))
        for i, (block, target) in enumerate(blocks):
            tails.append(pltpu.make_async_copy(block, target, tsem.at[side, i]))
    for copy in tails:
        copy.start()
    for par in range(2):
        @pl.when(used[par] > 0)
        def _():
            drain(par)
    for m in range(7, 13):
        @pl.when(m >= total)
        def _():
            pltpu.make_async_copy(zero, zero, zsem.at[m - 7]).wait()
    for copy in tails:
        copy.wait()


def run_step(counts, labels, images, own, weights, head):
    hbm = pl.BlockSpec(memory_space=pl.ANY)
    smem = pl.BlockSpec(memory_space=pltpu.SMEM)
    shapes = [jax.ShapeDtypeStruct((16, rows, HALF), F32) for rows in (128, 128, 96, 96)] * 2
    return pl.pallas_call(
        step_kernel,
        in_specs=[smem, smem] + [hbm] * 24,
        out_specs=[hbm] * 8,
        out_shape=shapes,
        scratch_shapes=[
            pltpu.VMEM((4, 4, CHAN, CHAN), BF16),
            pltpu.VMEM((4, 4, 16, CHAN), BF16),
            pltpu.VMEM((14, POS, CHAN), BF16),
            pltpu.VMEM((13, POS, CHAN), BF16),
            pltpu.VMEM((4, 20, 32, LANE), F32),
            pltpu.VMEM((POS, CHAN), BF16),
            pltpu.VMEM((2, 16, 2, 16, CHAN), F32),
            pltpu.VMEM((16, 2, 16, CHAN), F32),
            pltpu.VMEM((13, 16, CHAN), F32),
            pltpu.VMEM((16, 2, 16, LANE), F32),
            pltpu.VMEM((CLASSES, CHAN), F32),
            pltpu.SemaphoreType.DMA((4,)),
            pltpu.SemaphoreType.DMA((4,)),
            pltpu.SemaphoreType.DMA,
            pltpu.SemaphoreType.DMA,
            pltpu.SemaphoreType.DMA((2,)),
            pltpu.SemaphoreType.DMA((6,)),
            pltpu.SemaphoreType.DMA((2, 3)),
        ],
        compiler_params=pltpu.CompilerParams(vmem_limit_bytes=56 * 1024 * 1024),
        name="step",
    )(counts, labels, images, own, *weights, head)


def finish_kernel(counts, r0, r1, r2, r3, grad_pointwise, grad_depthwise, turned):
    seg = lax.axis_index("segment")
    total = counts[0] + counts[1] + counts[2] + counts[3]
    base = jnp.int32(0)
    for s in range(3):
        base = base + jnp.where(s < seg, counts[s], 0)
    here = counts[seg]
    rows = r0[...] + r1[...] + r2[...] + r3[...]
    for j in range(4):
        grad_pointwise[j] = jnp.where(j < here, rows[48 - 16 * j:64 - 16 * j, :], 0.0)
    taps = rows[64:80, 0:LANE]
    turned[...] = jnp.transpose(taps)
    for j in range(4):
        first = jnp.maximum(total - 1 - base - j, 0) * 9
        grad_depthwise[:, j, :] = jnp.where(j < here, turned[pl.ds(first, 9), :], 0.0)


def finish(counts, parts):
    vmem = pl.BlockSpec(memory_space=pltpu.VMEM)
    return pl.pallas_call(
        finish_kernel,
        in_specs=[pl.BlockSpec(memory_space=pltpu.SMEM)] + [vmem] * 4,
        out_specs=[vmem, vmem],
        out_shape=[jax.ShapeDtypeStruct((4, 16, CHAN), F32), jax.ShapeDtypeStruct((9, 4, 16), F32)],
        scratch_shapes=[pltpu.VMEM((LANE, 16), F32)],
        name="finish",
    )(counts, *parts)


def rotate(k):
    return [(i, (i + k) % 4) for i in range(4)]


def along(axis, k):
    if axis == "x":
        return "segment", rotate(k)
    pairs = []
    for d in range(32):
        y, z, c = d // 8, d // 2 % 4, d % 2
        if axis == "y":
            y = (y + k) % 4
        elif axis == "z":
            z = (z + k) % 4
        else:
            c = c ^ 1
        pairs.append((d, y * 8 + z * 2 + c))
    return "dp", pairs


def move(value, axis, k=1):
    name, pairs = along(axis, k)
    return lax.ppermute(value, name, pairs)


def gather_weights(pointwise, depthwise, place):
    core, my_z = place["core"], place["z"]
    taps = jnp.pad(depthwise, ((0, 0), (0, 7), (0, 0)))
    direct = lax.dynamic_index_in_dim(pointwise, core, 0, keepdims=False)
    shared = lax.dynamic_slice(pointwise, (2 + core, my_z * 128, 0), (1, 128, CHAN))
    piece = jnp.concatenate([shared[0], taps.reshape(64, CHAN)], axis=0)
    pieces = [move(piece, "x", k) for k in (1, 2, 3)]
    *pieces, direct = lax.optimization_barrier([*pieces, direct])
    whole = [move(direct, "x", 1), None, move(direct, "x", 3)]
    stacked = jnp.stack([p[0:128] for p in pieces])
    near = [move(stacked, "z", 1), None, move(stacked, "z", 3)]
    swapped = move(stacked, "core")
    whole[1:2] = [move(whole[0][0:256], "x", 1), move(whole[2][256:512], "x", 3)]
    near[1:2] = [move(near[0][:, 0:64], "z", 1), move(near[2][:, 64:128], "z", 3)]
    other = [move(part, "core") for part in whole]
    far = [move(part, "core") for part in near]
    return [taps, *pieces, *whole, *other, swapped, *near, *far]


def pick(value, place, axis, dim, k):
    return lax.dynamic_index_in_dim(value, (place[axis] + k) % 4, dim, keepdims=False)


def reduce_halves(keeps, sends, orders, place):
    received = [move(send, "core") for send in sends]
    pieces = []
    for q, order in enumerate(orders):
        axis, dim = order[0], "yz".index(order[0])
        cut = {}
        for h in (0, 1):
            keep, extra = (v[2 * q + h].reshape(4, 4, COLOR_ROWS[q], HALF) for v in (keeps, received))
            for k in (2, 1, 3, 0):
                cut[k, h] = pick(keep, place, axis, dim, k) + pick(extra, place, axis, dim, k)
        pieces.append(lax.optimization_barrier(cut))
    first = [{} for _ in pieces]
    for k, h, step in ((2, 0, 1), (2, 1, 3), (1, 1, 1), (3, 0, 3)):
        for q, order in enumerate(orders):
            first[q][k, h] = move(pieces[q][k, h], order[0], step)
    second = [{(1, 0): pieces[q][1, 0] + first[q][2, 0], (3, 1): pieces[q][3, 1] + first[q][2, 1]} for q in (0, 1)]
    second = [lax.optimization_barrier(part) for part in second]
    last = [{} for _ in pieces]
    for k, h in ((1, 0), (3, 1)):
        for q, order in enumerate(orders):
            last[q][k, h] = move(second[q][k, h], order[0], k)
    first, last = lax.optimization_barrier((first, last))
    values = []
    for q in (0, 1):
        low = pieces[q][0, 0] + last[q][1, 0] + first[q][3, 0]
        high = pieces[q][0, 1] + first[q][1, 1] + last[q][3, 1]
        values.append(jnp.concatenate([low, high], axis=2))
    values = [lax.optimization_barrier(value) for value in values]
    pieces = [[pick(value, place, order[1], 0, k) for k in range(4)] for value, order in zip(values, orders)]
    pieces = [lax.optimization_barrier(part) for part in pieces]
    moved = [[own[0]] for own in pieces]
    for k in (2, 1, 3):
        for q, order in enumerate(orders):
            moved[q].append(move(pieces[q][k], order[1], k))
    moved = lax.optimization_barrier(moved)
    return [m[0] + m[1] + m[2] + m[3] for m in moved]


def local(images, labels, counts, depthwise, pointwise, head_weight):
    seg = lax.axis_index("segment")
    dp = lax.axis_index("dp")
    place = {"x": seg, "y": dp // 8, "z": dp // 2 % 4, "core": dp % 2}
    weights = gather_weights(pointwise, depthwise, place)
    outs = run_step(counts, labels, images.reshape(4, POS, CHAN), pointwise, weights, head_weight.T)
    sums = reduce_halves(outs[:4], outs[4:], ("yz", "zy"), place)
    ordered = jnp.concatenate([jnp.zeros((48, CHAN), F32), *sums], axis=0)
    total = jnp.sum(counts)
    before = jnp.cumsum(counts) - counts
    taps_rows = ordered[256:272]
    parts = []
    for k in range(4):
        dest = (seg + k) % 4
        start = (total - 1 - lax.dynamic_index_in_dim(before, dest, 0, keepdims=False)) * 16
        piece = jnp.concatenate([lax.dynamic_slice_in_dim(ordered, start, 64, 0), taps_rows], axis=0)
        parts.append(move(piece, "x", k) if k else piece)
    grad_pointwise, grad_depthwise = finish(counts, parts)
    return grad_pointwise, jnp.transpose(grad_depthwise, (1, 0, 2))


def solution(mesh):
    in_specs = (P("dp", None, None, None), P("dp"), P(), P("segment", None, None), P("segment", None, None), P())
    out_specs = (P("segment", "dp", None), P("segment", None, "dp"))
    return jax.shard_map(local, mesh=mesh, in_specs=in_specs, out_specs=out_specs, check_vma=False)
```
